1024 devices in a mesh: dp: 4 (over y_lo, core), expert: 32 (over z), tpin: 2 (over y_hi), tpout: 4 (over x).
Axes of the slice: x: 4, y: 4 (y_hi: 2, y_lo: 2; y = y_hi * 2 + y_lo), z: 32, core: 2. Of those that a mesh axis runs over, the one named last changes fastest.
Arguments:
- tokens: bfloat16 [512, 6144], P('expert', ('dp', 'tpin', 'tpout')), may hold values from -6 to 6
- cotangent: bfloat16 [512, 6144], P('expert', ('dp', 'tpin', 'tpout')), may hold values from -6 to 6
- expert_ids: int32 [512, 2], P('expert'), may hold values from 0 to 7, all different within a row; in each aligned block of 16 rows (0 to 15, 16 to 31, ...) at most 6 rows name the same one
- gate_weights: float32 [512, 2], P('expert'), may hold values from 0.25 to 1
- w_gate: bfloat16 [6144, 65536], P(('dp', 'tpin'), ('expert', 'tpout')), may hold values from -0.078125 to 0.078125
- w_up: bfloat16 [6144, 65536], P(('dp', 'tpin'), ('expert', 'tpout')), may hold values from -0.078125 to 0.078125
- w_down: bfloat16 [65536, 6144], P(('expert', 'tpout'), ('dp', 'tpin')), may hold values from -0.0625 to 0.0625
Outputs:
- layer_out: bfloat16 [512, 6144], P('expert', ('dp', 'tpin', 'tpout'))
- token_grad: bfloat16 [512, 6144], P('expert', ('dp', 'tpin', 'tpout'))
- down_grad: bfloat16 [65536, 6144], P(('expert', 'tpout'), ('dp', 'tpin'))
The draws below stay inside these ranges and needn't reach their ends.
Inputs may be any that keep to these rules, and one draw needn't show every extreme that they name: `expert_ids`: each row names 2 different experts. In each aligned block of 16 rows no expert is named by more than 6 rows, a bound that some block reaches.
All inputs are finite; a program needn't handle non-finite values.
Results may differ from the reference program's by a relative error of at most 0.0057.
Values may be sent and summed in bfloat16 or wider, within the bound.
A program may use at most 64 MiB of HBM per device.

```python
import math
import jax
import jax.numpy as jnp
import numpy as np
from jax import lax

D = 6144
EXPERTS = 8
HID = 8192
TOP = 2
TOK_G = 16
CAP = 6
TOKENS = 512
N_EXPERT = 32


def levels(own_key, dims, split, smallest, largest):
    factor_of, own = 1.0, jax.random.fold_in(own_key, 6)
    for dim, blocks in split:
        steps = jnp.exp(jax.random.uniform(jax.random.fold_in(own, dim), (blocks,), jnp.float32, smallest / len(split), largest / len(split)))
        factor_of = factor_of * jnp.repeat(steps, dims[dim] // blocks).reshape([-1 if axis == dim else 1 for axis in range(len(dims))])
    return factor_of


def shared_out(own_key, own, number, rows, amount, top, reach, skew):
    order = jax.random.permutation(own_key, amount)
    heavy_load, usual = portions_of(amount, rows * top, reach, skew, True), portions_of(amount, rows * top, reach, skew, False)
    places = jnp.arange(amount)

    def named(tallies, rotation):
        used = int((tallies > 0).sum())
        fixed = max(1, used // 4)
        moved = fixed + (places - fixed + rotation * (used - fixed)) % max(1, amount - fixed)
        return jnp.zeros((amount,), jnp.int32).at[order[jnp.where(places < fixed, places, moved)]].set(jnp.asarray(tallies, jnp.int32))

    tallies = jnp.where(number % 4 == 0, named(heavy_load, number // 4), named(usual, number - number // 4 - 1))
    mixed = jax.random.permutation(jax.random.fold_in(own, 3), amount)
    giver, taker = mixed[0:amount // 2 * 2:2], mixed[1:amount // 2 * 2:2]
    room = jnp.minimum(tallies[giver] - 1, reach - tallies[taker]) // 2
    room = jnp.where((giver == order[0]) | (taker == order[0]) | (tallies[taker] == 0), 0, jnp.maximum(room, 0))
    moved = jax.random.randint(jax.random.fold_in(own, 4), (amount // 2,), 0, 1 << 20) % (room + 1)
    tallies = tallies.at[giver].add(-moved).at[taker].add(moved)
    members = jnp.searchsorted(jnp.cumsum(tallies), jnp.arange(rows * top), side="right").astype(jnp.int32)
    grid = members.reshape(top, rows).T
    grid = grid[jax.random.permutation(jax.random.fold_in(own, 1), rows)]
    rotation = jax.random.randint(jax.random.fold_in(own, 2), (rows, 1), 0, top)
    return jnp.take_along_axis(grid, (jnp.arange(top)[None, :] + rotation) % top, axis=1)


def portions_of(number_of, total, bound, slope, full):
    portions = [(1 << 20) // math.isqrt(grade ** slope) + 1 for grade in range(1, number_of + 1)]
    largest = bound if full else min(bound, max(-(-total // number_of), total * portions[0] // sum(portions)))
    least = 1 if total - largest >= number_of - 1 else 0
    counts, surplus = [largest] + [least] * (number_of - 1), total - largest - least * (number_of - 1)
    while surplus > 0:
        candidates = [i for i in range(1, number_of) if counts[i] < largest] or [i for i in range(1, number_of) if counts[i] < bound]
        pool, budget = sum([portions[i] for i in candidates]), surplus
        for i in candidates:
            addition = min(bound - counts[i], max(1, budget * portions[i] // pool), surplus)
            counts[i] = counts[i] + addition
            surplus = surplus - addition
    return np.array(counts)


def scatter_about(rng, shape, deviation, most, cuts=(), kind=jnp.bfloat16):
    loudness = levels(rng, shape, cuts, -0.22, 0.18) if cuts else 1.0
    drawn = jax.random.normal(rng, shape, jnp.float32) * deviation * loudness
    return jnp.minimum(jnp.maximum(drawn, -most), most).astype(kind)


def setup_inputs(seed: int = 0) -> dict:
    keys = jax.random.split(jax.random.key(seed), 8)
    tokens = scatter_about(keys[0], (TOKENS, D), 1.0, 6.0, ((0, 32), (1, 32)))
    cotangent = scatter_about(keys[1], (TOKENS, D), 1.0, 6.0, ((0, 32), (1, 32)))
    expert_ids_keys = jax.random.split(jax.random.fold_in(keys[2], 1), TOKENS // TOK_G)
    expert_ids_turns = jax.random.permutation(jax.random.fold_in(keys[2], 3), TOKENS // TOK_G)
    expert_ids = jax.vmap(lambda own, number: shared_out(jax.random.fold_in(keys[2], 2), own, number, TOK_G, EXPERTS, TOP, CAP, 1))(expert_ids_keys, expert_ids_turns).reshape((TOKENS, TOP))
    gate_weights = jnp.clip(0.25 + 0.75 * jax.random.uniform(keys[3], (TOKENS, TOP), jnp.float32) ** levels(keys[3], (TOKENS, TOP), ((0, 32),), -0.2, 0.2), 0.25, 1.0)
    w_gate = scatter_about(keys[4], (D, EXPERTS * HID), D ** -0.5, 0.078125, ((0, 8), (1, 128)))
    w_up = scatter_about(keys[5], (D, EXPERTS * HID), D ** -0.5, 0.078125, ((0, 8), (1, 128)))
    w_down = scatter_about(keys[6], (EXPERTS * HID, D), HID ** -0.5, 0.0625, ((0, 128), (1, 8)))
    return {"tokens": tokens, "cotangent": cotangent, "expert_ids": expert_ids, "gate_weights": gate_weights, "w_gate": w_gate, "w_up": w_up, "w_down": w_down}


def reference(tokens, cotangent, expert_ids, gate_weights, w_gate, w_up, w_down):
    route_rows = N_EXPERT * CAP
    model_width = tokens.shape[1]

    def expert_step(carry, expert):
        out_acc, grad_acc = carry
        hit = expert_ids == expert
        weight = jnp.sum(jnp.where(hit, gate_weights, jnp.zeros_like(gate_weights)), axis=1)
        routed = jnp.any(hit, axis=1)
        order = jnp.argsort(jnp.logical_not(routed).astype(jnp.int32), stable=True)[:route_rows].astype(jnp.int32)
        x_rows = tokens[order]
        weight_rows = weight[order]
        start = (expert * HID).astype(jnp.int32)
        gate_cols = lax.dynamic_slice_in_dim(w_gate, start, HID, 1)
        up_cols = lax.dynamic_slice_in_dim(w_up, start, HID, 1)
        down_rows = lax.dynamic_slice_in_dim(w_down, start, HID, 0)
        gate = jnp.dot(x_rows, gate_cols, preferred_element_type=jnp.float32)
        up = jnp.dot(x_rows, up_cols, preferred_element_type=jnp.float32)
        sig = jax.nn.sigmoid(gate)
        hidden = (gate * sig * up).astype(jnp.bfloat16)
        expert_out = jnp.dot(hidden, down_rows, preferred_element_type=jnp.float32)
        out_acc = out_acc.at[order].add(weight_rows[:, None] * expert_out)
        routed_grad = (weight_rows[:, None] * cotangent[order].astype(jnp.float32)).astype(jnp.bfloat16)
        hidden_grad = jnp.dot(routed_grad, down_rows.T, preferred_element_type=jnp.float32)
        gate_grad = (hidden_grad * up * sig * (1.0 + gate * (1.0 - sig))).astype(jnp.bfloat16)
        up_grad = (hidden_grad * gate * sig).astype(jnp.bfloat16)
        row_grad = jnp.dot(gate_grad, gate_cols.T, preferred_element_type=jnp.float32) + jnp.dot(up_grad, up_cols.T, preferred_element_type=jnp.float32)
        grad_acc = grad_acc.at[order].add(row_grad)
        down_part = jnp.dot(hidden.T, routed_grad, preferred_element_type=jnp.float32).astype(jnp.bfloat16)
        return (out_acc, grad_acc), down_part

    start_acc = jnp.zeros((tokens.shape[0], model_width), jnp.float32)
    (out_acc, grad_acc), down_parts = lax.scan(expert_step, (start_acc, start_acc), jnp.arange(EXPERTS, dtype=jnp.int32))
    down_grad = down_parts.reshape(EXPERTS * HID, model_width)
    return out_acc.astype(jnp.bfloat16), grad_acc.astype(jnp.bfloat16), down_grad
```

```python
import jax
import jax.numpy as jnp
from jax import lax
from jax.experimental import pallas as pl
from jax.experimental.pallas import tpu as pltpu
from jax.sharding import PartitionSpec as P

EXPERTS = 8
HID = 8192
CAP = 6
SLOT = 8
MESH = pl.DeviceIdType.MESH
F32 = jnp.float32
BF16 = jnp.bfloat16

HOPS = (0, 1, 2, 3, 4, 3, 2, 1)
AHEAD = (0, 1, 1, 1, 0, -1, -1, -1)
FIRST = (4, 3, 5, 2, 6, 1, 7)
RELAYS = tuple((k, h) for h in (1, 2, 3) for k in (4, 3, 5, 2, 6) if HOPS[k] > h)
ARRIVALS = tuple((k, h) for k in range(1, 8) for h in range(1, HOPS[k] + 1))


def dot(a, b, contract=((1,), (0,)), precision=None):
    return lax.dot_general(
        a, b, (contract, ((), ())), preferred_element_type=F32, precision=precision
    )


def kernel(
    ids_ref, gw_ref, tok_ref, cot_ref, wg_hbm, wu_hbm, wd_hbm,
    out_ref, grad_ref, down_hbm,
    wg, wu, wd, w_sem,
    a_src, a_relay, a_dst, a_send, a_recv,
    xg, b_zsend, b_zrecv, b_xsend, b_xrecv,
    p_mine, d1_src, d1_dst, d1_send, d1_recv,
    d2_src, d2_dst, d2_send, d2_recv,
    h_all, d3_send, d3_recv, d4_send, d4_recv,
    f_mine, f_src, f_dst, f_send, f_recv,
    z_src, z_dst, z_send, z_recv,
    g_src, g_dst, g_send, g_recv,
    down_buf, down_sem,
):
    z = lax.axis_index("expert")
    x = lax.axis_index("tpout")
    y_hi = lax.axis_index("tpin")
    dp = lax.axis_index("dp")
    planes = lax.axis_size("expert") // EXPERTS
    group, plane = z // planes, z % planes
    core = dp % 2
    y = y_hi * 2 + dp // 2
    side = 1 - 2 * core
    xs = lax.axis_size("tpout")

    def at_group(step):
        return {"expert": ((group + step + EXPERTS) % EXPERTS) * planes + plane}

    def at_plane(p):
        return {"expert": group * planes + p}

    def at_x(step):
        return {"tpout": (x + step + xs) % xs}

    def at_y(step):
        there = (y + step + 4) % 4
        return {"tpin": there // 2, "dp": (there % 2) * 2 + core}

    partner = {"dp": dp + side}
    near_planes = (plane + 1 - 2 * (plane % 2), (plane + 2) % 4, 3 - plane)

    def remote(src, dst, send, recv, device):
        return pltpu.make_async_remote_copy(
            src_ref=src, dst_ref=dst, send_sem=send, recv_sem=recv,
            device_id=device, device_id_type=MESH,
        )

    barrier = pltpu.get_barrier_semaphore()
    peers = [at_group(1), at_group(-1), at_x(1), at_x(-1), at_y(1), at_y(-1), partner]
    peers += [at_plane(p) for p in near_planes]
    for peer in peers:
        pl.semaphore_signal(barrier, inc=1, device_id=peer, device_id_type=MESH)
    weights = [
        pltpu.make_async_copy(src, dst, w_sem.at[i])
        for i, (src, dst) in enumerate(((wg_hbm, wg), (wu_hbm, wu), (wd_hbm, wd)))
    ]
    for copy in weights:
        copy.start()

    ahead = (ids_ref[...] + EXPERTS - group) % EXPERTS
    gw = gw_ref[...]
    tokens_n = ahead.shape[1]
    expert_row = lax.broadcasted_iota(jnp.int32, (EXPERTS, tokens_n), 0)
    hit0 = jnp.where(expert_row == ahead[0:1, :], 1.0, 0.0).astype(F32)
    hit1 = jnp.where(expert_row == ahead[1:2, :], 1.0, 0.0).astype(F32)
    hit = hit0 + hit1
    weight = hit0 * gw[0:1, :] + hit1 * gw[1:2, :]
    before = jnp.where(
        lax.broadcasted_iota(jnp.int32, (tokens_n, tokens_n), 0)
        < lax.broadcasted_iota(jnp.int32, (tokens_n, tokens_n), 1), 1.0, 0.0
    ).astype(F32)
    rank = dot(hit, before)

    def spread(v):
        return jnp.concatenate(
            [jnp.broadcast_to(v[e : e + 1, :], (SLOT, tokens_n)) for e in range(EXPERTS)], axis=0
        )

    slots_n = EXPERTS * SLOT
    slot_j = (lax.broadcasted_iota(jnp.int32, (slots_n, tokens_n), 0) % SLOT).astype(F32)
    chosen = jnp.where(spread(rank) == slot_j, spread(hit), 0.0)
    slot_weights = chosen * spread(weight)
    chosen_b = chosen.astype(BF16)
    slot_gate = jnp.sum(slot_weights, axis=1, keepdims=True)
    x_rows = dot(chosen_b, tok_ref[...])
    dy_rows = dot(chosen_b, cot_ref[...]) * slot_gate
    feat = x_rows.shape[1]
    both = jnp.concatenate([x_rows, dy_rows], axis=1)
    a_src[...] = both.reshape(EXPERTS, SLOT, 2 * feat).astype(BF16)
    a_dst[0] = a_src[0]

    pl.semaphore_wait(barrier, len(peers))

    def a_copy(k, h):
        src = a_src.at[k] if h == 1 else a_relay.at[RELAYS.index((k, h - 1))]
        dst = a_dst.at[k] if h == HOPS[k] else a_relay.at[RELAYS.index((k, h))]
        n = ARRIVALS.index((k, h))
        step = side if k == 4 else AHEAD[k]
        return remote(src, dst, a_send.at[n], a_recv.at[n], at_group(step))

    for k in FIRST:
        a_copy(k, 1).start()
    chosen_t = chosen.T
    weights_t = slot_weights.T
    for k, h in RELAYS:
        a_copy(k, h).wait_recv()
        a_copy(k, h + 1).start()
    for k in range(1, 8):
        a_copy(k, HOPS[k]).wait_recv()

    cap_rows = EXPERTS * CAP

    def squeeze(shape, long_axis):
        rows = lax.broadcasted_iota(jnp.int32, shape, long_axis)
        short = lax.broadcasted_iota(jnp.int32, shape, 1 - long_axis)
        return jnp.where(short // CAP * SLOT + short % CAP == rows, 1.0, 0.0).astype(BF16)

    arrived = a_dst[...].reshape(slots_n, 2 * feat)
    xg[x, plane] = dot(squeeze((cap_rows, slots_n), 1), arrived).astype(BF16)

    order = (plane,) + near_planes

    def bz_out(j):
        mine = xg.at[x, plane]
        return remote(mine, mine, b_zsend.at[j - 1], b_zrecv.at[j - 1], at_plane(order[j]))

    def bz_in(j):
        there = xg.at[x, order[j]]
        return remote(there, there, b_zsend.at[j - 1], b_zrecv.at[j - 1], at_plane(order[j]))

    def bx_out(j, way):
        mine = xg.at[x, order[j]]
        n = 0 if way == 1 else 1
        return remote(mine, mine, b_xsend.at[j, n], b_xrecv.at[j, n], at_x(way))

    def bx_in(j, way):
        there = xg.at[(x - way + xs) % xs, order[j]]
        n = 0 if way == 1 else 1
        return remote(there, there, b_xsend.at[j, n], b_xrecv.at[j, n], at_x(way))

    def bx_pass(j):
        way = 1 if j < 2 else -1
        there = xg.at[(x - way + xs) % xs, order[j]]
        return remote(there, there, b_xsend.at[j, 2], b_xrecv.at[j, 2], at_x(way))

    def bx_far(j):
        there = xg.at[(x + 2) % xs, order[j]]
        return remote(there, there, b_xsend.at[j, 2], b_xrecv.at[j, 2], at_x(1))

    for j in (1, 2, 3):
        bz_out(j).start()
    for way in (1, -1):
        bx_out(0, way).start()

    def relay_x(j):
        bx_in(j, 1 if j < 2 else -1).wait_recv()
        bx_pass(j).start()

    for j in (1, 2, 3):
        bz_in(j).wait_recv()
        for way in (1, -1):
            bx_out(j, way).start()
        relay_x(j - 1)
    relay_x(3)
    for copy in weights:
        copy.wait()
    for j in range(4):
        bx_in(j, -1 if j < 2 else 1).wait_recv()
        bx_far(j).wait_recv()

    rows_n = planes * cap_rows
    half = rows_n // 2
    blocks = [xg[i].reshape(rows_n, 2 * feat) for i in range(4)]
    x_all = jnp.concatenate([b[:, :feat] for b in blocks], axis=1)
    dy_all = jnp.concatenate([b[:, feat:] for b in blocks], axis=1)
    parts = (
        dot(x_all, wg[...]),
        dot(x_all, wu[...]),
        dot(dy_all, wd[...], ((1,), (1,))),
    )
    for i in range(4):
        for n, part in enumerate(parts):
            p_mine[i, :, n * 128 : (n + 1) * 128] = part[:, i * 128 : (i + 1) * 128]

    my_rows = pl.ds(pl.multiple_of(core * half, half), half)
    its_rows = pl.ds(pl.multiple_of((1 - core) * half, half), half)

    def d1(i):
        return remote(d1_src.at[i], d1_dst.at[i], d1_send.at[i], d1_recv.at[i], partner)

    wrap_y = [(y + step) % 4 for step in range(4)]
    for step in (2, 1, 3, 0):
        d1_src[step] = p_mine[wrap_y[step], its_rows, :].astype(BF16)
        d1(step).start()

    quarter = half // 2
    top, bottom = pl.ds(0, quarter), pl.ds(quarter, quarter)

    def d2(n, way):
        return remote(d2_src.at[n], d2_dst.at[n], d2_send.at[n], d2_recv.at[n], at_y(way))

    def pair_sum(step):
        d1(step).wait_recv()
        return p_mine[wrap_y[step], my_rows, :] + d1_dst[step].astype(F32)

    far = pair_sum(2).astype(BF16)
    d2_src[0] = far[:quarter]
    d2(0, 1).start()
    d2_src[1] = far[quarter:]
    d2(1, -1).start()
    ahead_sum = pair_sum(1)
    d2_src[2] = ahead_sum[quarter:].astype(BF16)
    d2(2, 1).start()
    back_sum = pair_sum(3)
    d2_src[3] = back_sum[:quarter].astype(BF16)
    d2(3, -1).start()
    mine = pair_sum(0)
    d2(0, 1).wait_recv()
    d2_src[4] = (ahead_sum[:quarter] + d2_dst[0].astype(F32)).astype(BF16)
    d2(4, 1).start()
    d2(1, -1).wait_recv()
    d2_src[5] = (back_sum[quarter:] + d2_dst[1].astype(F32)).astype(BF16)
    d2(5, -1).start()
    for n, way in ((2, 1), (3, -1), (4, 1), (5, -1)):
        d2(n, way).wait_recv()
    from_back = jnp.concatenate([d2_dst[4], d2_dst[2]], axis=0).astype(F32)
    from_ahead = jnp.concatenate([d2_dst[3], d2_dst[5]], axis=0).astype(F32)
    total = mine + from_back + from_ahead

    gate, up, hidden_grad = total[:, :128], total[:, 128:256], total[:, 256:]
    sig = 1.0 / (1.0 + jnp.exp(-gate))
    hidden = (gate * sig * up).astype(BF16)
    gate_grad = (hidden_grad * up * sig * (1.0 + gate * (1.0 - sig))).astype(BF16)
    up_grad = (hidden_grad * gate * sig).astype(BF16)
    h_all[y, core] = jnp.concatenate([hidden, gate_grad, up_grad], axis=1)

    def d3_out(way):
        own = h_all.at[y, core]
        n = 0 if way == 1 else 1
        return remote(own, own, d3_send.at[n], d3_recv.at[n], at_y(way))

    def d3_in(way):
        there = h_all.at[(y - way + 4) % 4, core]
        n = 0 if way == 1 else 1
        return remote(there, there, d3_send.at[n], d3_recv.at[n], at_y(way))

    def d3_pass(way):
        n, rows = (2, top) if way == 1 else (3, bottom)
        there = h_all.at[(y - way + 4) % 4, core, rows]
        return remote(there, there, d3_send.at[n], d3_recv.at[n], at_y(way))

    def d3_far(way):
        n, rows = (2, top) if way == 1 else (3, bottom)
        there = h_all.at[(y + 2) % 4, core, rows]
        return remote(there, there, d3_send.at[n], d3_recv.at[n], at_y(way))

    def d4(step, whose):
        there = h_all.at[wrap_y[step], whose]
        return remote(there, there, d4_send.at[step], d4_recv.at[step], partner)

    d3_out(1).start()
    d3_out(-1).start()
    d4(0, core).start()
    d3_in(1).wait_recv()
    d3_pass(1).start()
    d3_in(-1).wait_recv()
    d3_pass(-1).start()
    d4(3, core).start()
    d4(1, core).start()
    d3_far(1).wait_recv()
    d3_far(-1).wait_recv()
    d4(2, core).start()
    for step in range(4):
        d4(step, 1 - core).wait_recv()

    acts = [h_all[i].reshape(rows_n, 384) for i in range(4)]
    hidden_all = jnp.concatenate([a[:, :128] for a in acts], axis=1)
    gate_grad_all = jnp.concatenate([a[:, 128:256] for a in acts], axis=1)
    up_grad_all = jnp.concatenate([a[:, 256:] for a in acts], axis=1)
    out_rows = dot(hidden_all, wd[...])
    grad_rows = dot(gate_grad_all, wg[...], ((1,), (1,))) + dot(
        up_grad_all, wu[...], ((1,), (1,))
    )
    for i in range(4):
        cols = slice(i * feat, (i + 1) * feat)
        f_mine[i] = jnp.concatenate([out_rows[:, cols], grad_rows[:, cols]], axis=1)

    def f(n, way):
        return remote(f_src.at[n], f_dst.at[n], f_send.at[n], f_recv.at[n], at_x(way))

    def f_part(step):
        return f_mine[(x + step) % xs]

    far = f_part(2).astype(BF16)
    f_src[0] = far[:half]
    f(0, 1).start()
    f_src[1] = far[half:]
    f(1, -1).start()
    ahead_part = f_part(1)
    f_src[2] = ahead_part[half:].astype(BF16)
    f(2, 1).start()
    back_part = f_part(3)
    f_src[3] = back_part[:half].astype(BF16)
    f(3, -1).start()
    f(0, 1).wait_recv()
    f_src[4] = (ahead_part[:half] + f_dst[0].astype(F32)).astype(BF16)
    f(4, 1).start()
    f(1, -1).wait_recv()
    f_src[5] = (back_part[half:] + f_dst[1].astype(F32)).astype(BF16)
    f(5, -1).start()
    for n, way in ((2, 1), (3, -1), (4, 1), (5, -1)):
        f(n, way).wait_recv()
    from_back = jnp.concatenate([f_dst[4], f_dst[2]], axis=0).astype(F32)
    from_ahead = jnp.concatenate([f_dst[3], f_dst[5]], axis=0).astype(F32)
    f_mine[0] = f_part(0) + from_back + from_ahead

    def zc(j):
        return remote(z_src.at[j - 1], z_dst.at[j - 1], z_send.at[j - 1], z_recv.at[j - 1], at_plane(order[j]))

    def chunk(p):
        return pl.ds(pl.multiple_of(p * cap_rows, cap_rows), cap_rows)

    for j in (2, 3, 1):
        z_src[j - 1] = f_mine[0, chunk(order[j]), :].astype(BF16)
        zc(j).start()
    routes = f_mine[0, chunk(plane), :]
    for j in (1, 3, 2):
        zc(j).wait_recv()
        routes = routes + z_dst[j - 1].astype(F32)

    wide = dot(squeeze((slots_n, cap_rows), 0), routes.astype(BF16))
    g_src[...] = wide.reshape(EXPERTS, SLOT, 2 * feat).astype(BF16)

    def gc(k, way):
        return remote(g_src.at[k], g_dst.at[k], g_send.at[k - 1], g_recv.at[k - 1], at_group(way * k))

    for k in (4, 3, 5, 2, 6, 1, 7):
        gc(k, -1).start()
    g_dst[0] = g_src[0]
    down_buf[...] = dot(hidden_all, dy_all, ((0,), (0,))).astype(BF16)
    down_copy = pltpu.make_async_copy(down_buf, down_hbm, down_sem)
    down_copy.start()
    for k in range(1, 8):
        gc(k, 1).wait_recv()
    home = g_dst[...].reshape(slots_n, 2 * feat).astype(F32)
    out_ref[...] = dot(weights_t, home[:, :feat], precision=lax.Precision.HIGHEST).astype(BF16)
    grad_ref[...] = dot(chosen_t, home[:, feat:], precision=lax.Precision.HIGHEST).astype(BF16)

    down_copy.wait()
    for k in range(1, 8):
        for h in range(1, HOPS[k] + 1):
            a_copy(k, h).wait_send()
        gc(k, -1).wait_send()
    for j in (1, 2, 3):
        bz_out(j).wait_send()
        zc(j).wait_send()
    for j in range(4):
        bx_out(j, 1).wait_send()
        bx_out(j, -1).wait_send()
        bx_pass(j).wait_send()
        d1(j).wait_send()
        d4(j, core).wait_send()
    for n in range(6):
        d2(n, 1).wait_send()
        f(n, 1).wait_send()
    for way in (1, -1):
        d3_out(way).wait_send()
        d3_pass(way).wait_send()


def per_device(tokens, cotangent, expert_ids, gate_weights, w_gate, w_up, w_down):
    tok_rows, feat = tokens.shape
    wide, units = w_gate.shape
    planes = lax.axis_size("expert") // EXPERTS
    cap_rows = EXPERTS * CAP
    rows = planes * cap_rows
    half, quarter = rows // 2, rows // 4
    vmem = pl.BlockSpec(memory_space=pltpu.VMEM)
    hbm = pl.BlockSpec(memory_space=pl.ANY)
    dma = pltpu.SemaphoreType.DMA
    block = (EXPERTS, SLOT, 2 * feat)
    return pl.pallas_call(
        kernel,
        out_shape=(
            jax.ShapeDtypeStruct((tok_rows, feat), BF16),
            jax.ShapeDtypeStruct((tok_rows, feat), BF16),
            jax.ShapeDtypeStruct((units, wide), BF16),
        ),
        in_specs=[vmem, vmem, vmem, vmem, hbm, hbm, hbm],
        out_specs=(vmem, vmem, hbm),
        scratch_shapes=[
            pltpu.VMEM((wide, units), BF16), pltpu.VMEM((wide, units), BF16),
            pltpu.VMEM((units, wide), BF16), dma((3,)),
            pltpu.VMEM(block, BF16), pltpu.VMEM((len(RELAYS),) + block[1:], BF16),
            pltpu.VMEM(block, BF16), dma((len(ARRIVALS),)), dma((len(ARRIVALS),)),
            pltpu.VMEM((4, planes, cap_rows, 2 * feat), BF16),
            dma((3,)), dma((3,)), dma((4, 3)), dma((4, 3)),
            pltpu.VMEM((4, rows, 384), F32), pltpu.VMEM((4, half, 384), BF16),
            pltpu.VMEM((4, half, 384), BF16), dma((4,)), dma((4,)),
            pltpu.VMEM((6, quarter, 384), BF16), pltpu.VMEM((6, quarter, 384), BF16),
            dma((6,)), dma((6,)),
            pltpu.VMEM((4, 2, half, 384), BF16), dma((4,)), dma((4,)), dma((4,)), dma((4,)),
            pltpu.VMEM((4, rows, 2 * feat), F32), pltpu.VMEM((6, half, 2 * feat), BF16),
            pltpu.VMEM((6, half, 2 * feat), BF16), dma((6,)), dma((6,)),
            pltpu.VMEM((3, cap_rows, 2 * feat), BF16), pltpu.VMEM((3, cap_rows, 2 * feat), BF16),
            dma((3,)), dma((3,)),
            pltpu.VMEM(block, BF16), pltpu.VMEM(block, BF16), dma((7,)), dma((7,)),
            pltpu.VMEM((units, wide), BF16), dma,
        ],
        compiler_params=pltpu.CompilerParams(collective_id=0, has_side_effects=True),
    )(expert_ids.T, gate_weights.T, tokens, cotangent, w_gate, w_up, w_down)


def solution(mesh):
    return jax.shard_map(
        per_device,
        mesh=mesh,
        in_specs=(
            P("expert", ("dp", "tpin", "tpout")),
            P("expert", ("dp", "tpin", "tpout")),
            P("expert", None),
            P("expert", None),
            P(("dp", "tpin"), ("expert", "tpout")),
            P(("dp", "tpin"), ("expert", "tpout")),
            P(("expert", "tpout"), ("dp", "tpin")),
        ),
        out_specs=(
            P("expert", ("dp", "tpin", "tpout")),
            P("expert", ("dp", "tpin", "tpout")),
            P(("expert", "tpout"), ("dp", "tpin")),
        ),
        check_vma=False,
    )
```

```python
import jax
import jax.numpy as jnp
from jax import lax
from jax.experimental import pallas as pl
from jax.experimental.pallas import tpu as pltpu
from jax.sharding import PartitionSpec as P

EXPERTS = 8
HID = 8192
CAP = 6
SLOT = 8
MESH = pl.DeviceIdType.MESH
F32 = jnp.float32
BF16 = jnp.bfloat16

HOPS = (0, 1, 2, 3, 4, 3, 2, 1)
AHEAD = (0, 1, 1, 1, 0, -1, -1, -1)
FIRST = (4, 3, 5, 2, 6, 1, 7)
RELAYS = tuple((k, h) for h in (1, 2, 3) for k in (4, 3, 5, 2, 6) if HOPS[k] > h)
PLACE = (0, 1, 3, 5, 7, 6, 4, 2)
ARRIVALS = tuple((k, h) for k in range(1, 8) for h in range(1, HOPS[k] + 1))


def dot(a, b, contract=((1,), (0,)), precision=None):
    return lax.dot_general(
        a, b, (contract, ((), ())), preferred_element_type=F32, precision=precision
    )


def kernel(
    ids_hbm, gw_hbm, tok_hbm, cot_hbm, wg_hbm, wu_hbm, wd_hbm,
    home_hbm, slots_ref, hid_hbm, dy_hbm,
    ids_ref, gw_ref, tok_ref, cot_ref, in_sem,
    wg, wu, wd, w_sem,
    a_src, a_relay, a_dst, a_send, a_recv,
    xg, b_zsend, b_zrecv, b_xsend, b_xrecv,
    p_mine, d1_src, d1_dst, d1_send, d1_recv,
    d2_src, d2_dst, d2_send, d2_recv,
    h_all, d3_send, d3_recv, d4_send, d4_recv,
    f_mine, f_src, f_dst, f_send, f_recv,
    z_sum, z_src, z_dst, z_send, z_recv,
    g_src, g_send, g_recv,
    hid_buf, dy_buf, out_sem,
):
    sent = []

    z = lax.axis_index("expert")
    x = lax.axis_index("tpout")
    y_hi = lax.axis_index("tpin")
    dp = lax.axis_index("dp")
    planes = lax.axis_size("expert") // EXPERTS
    group, plane = z // planes, z % planes
    core = dp % 2
    y = y_hi * 2 + dp // 2
    side = 1 - 2 * core
    xs = lax.axis_size("tpout")

    def at_group(step):
        return {"expert": ((group + step + EXPERTS) % EXPERTS) * planes + plane}

    def at_plane(p):
        return {"expert": group * planes + p}

    def at_x(step):
        return {"tpout": (x + step + xs) % xs}

    def at_y(step):
        there = (y + step + 4) % 4
        return {"tpin": there // 2, "dp": (there % 2) * 2 + core}

    partner = {"dp": dp + side}
    near_planes = (plane + 1 - 2 * (plane % 2), (plane + 2) % 4, 3 - plane)

    def remote(src, dst, send, recv, device):
        return pltpu.make_async_remote_copy(
            src_ref=src, dst_ref=dst, send_sem=send, recv_sem=recv,
            device_id=device, device_id_type=MESH,
        )

    def start(copy):
        copy.start()
        sent.append(copy)

    barrier = pltpu.get_barrier_semaphore()
    peers = [at_group(1), at_group(-1), at_x(1), at_x(-1), at_y(1), at_y(-1), partner]
    peers += [at_plane(p) for p in near_planes]
    for peer in peers:
        pl.semaphore_signal(barrier, inc=1, device_id=peer, device_id_type=MESH)
    inputs = [
        pltpu.make_async_copy(src, dst, in_sem.at[i])
        for i, (src, dst) in enumerate(
            ((ids_hbm, ids_ref), (gw_hbm, gw_ref), (tok_hbm, tok_ref), (cot_hbm, cot_ref))
        )
    ]
    for copy in inputs:
        copy.start()
    weights = [
        pltpu.make_async_copy(src, dst, w_sem.at[i])
        for i, (src, dst) in enumerate(((wg_hbm, wg), (wu_hbm, wu), (wd_hbm, wd)))
    ]
    for copy in weights:
        copy.start()
    for copy in inputs:
        copy.wait()

    ahead = (ids_ref[...] + EXPERTS - group) % EXPERTS
    gw = gw_ref[...]
    tokens_n = ahead.shape[1]
    expert_row = lax.broadcasted_iota(jnp.int32, (EXPERTS, tokens_n), 0)
    hit0 = jnp.where(expert_row == ahead[0:1, :], 1.0, 0.0).astype(F32)
    hit1 = jnp.where(expert_row == ahead[1:2, :], 1.0, 0.0).astype(F32)
    hit = hit0 + hit1
    weight = hit0 * gw[0:1, :] + hit1 * gw[1:2, :]
    before = jnp.where(
        lax.broadcasted_iota(jnp.int32, (tokens_n, tokens_n), 0)
        < lax.broadcasted_iota(jnp.int32, (tokens_n, tokens_n), 1), 1.0, 0.0
    ).astype(F32)
    rank = dot(hit, before)

    def spread(v):
        return jnp.concatenate(
            [jnp.broadcast_to(v[e : e + 1, :], (SLOT, tokens_n)) for e in range(EXPERTS)], axis=0
        )

    slots_n = EXPERTS * SLOT
    slot_j = (lax.broadcasted_iota(jnp.int32, (slots_n, tokens_n), 0) % SLOT).astype(F32)
    chosen = jnp.where(spread(rank) == slot_j, spread(hit), 0.0)
    slot_weights = chosen * spread(weight)
    chosen_b = chosen.astype(BF16)
    slot_gate = jnp.sum(slot_weights, axis=1, keepdims=True)
    x_rows = dot(chosen_b, tok_ref[...])
    dy_rows = dot(chosen_b, cot_ref[...]) * slot_gate
    feat = x_rows.shape[1]
    both = jnp.concatenate([x_rows, dy_rows], axis=1)
    a_src[...] = both.reshape(EXPERTS, SLOT, 2 * feat).astype(BF16)
    a_dst[0] = a_src[0]

    slots_ref[0] = slot_weights
    slots_ref[1] = chosen

    pl.semaphore_wait(barrier, len(peers))

    def a_copy(k, h):
        src = a_src.at[k] if h == 1 else a_relay.at[RELAYS.index((k, h - 1))]
        dst = a_dst.at[PLACE[k]] if h == HOPS[k] else a_relay.at[RELAYS.index((k, h))]
        n = ARRIVALS.index((k, h))
        step = side if k == 4 else AHEAD[k]
        return remote(src, dst, a_send.at[n], a_recv.at[n], at_group(step))

    def a_pass(hop):
        for k, h in RELAYS:
            if h == hop:
                a_copy(k, h).wait_recv()
                start(a_copy(k, h + 1))

    cap_rows = EXPERTS * CAP
    part_rows = cap_rows // 2

    def squeeze(shape, long_axis):
        rows = lax.broadcasted_iota(jnp.int32, shape, long_axis)
        short = lax.broadcasted_iota(jnp.int32, shape, 1 - long_axis)
        return jnp.where(short // CAP * SLOT + short % CAP == rows, 1.0, 0.0).astype(BF16)

    order = (plane,) + near_planes

    def bz(c, j, whose):
        there = xg.at[x, whose, c]
        return remote(there, there, b_zsend.at[c, j - 1], b_zrecv.at[c, j - 1], at_plane(order[j]))

    def bx(c, j, n, step, way):
        there = xg.at[(x + step + xs) % xs, order[j], c]
        return remote(there, there, b_xsend.at[c, j, n], b_xrecv.at[c, j, n], at_x(way))

    def spread_x(c, j):
        start(bx(c, j, 0, 0, 1))
        start(bx(c, j, 1, 0, -1))

    def relay_x(c, j):
        n, way = (0, 1) if j < 2 else (1, -1)
        bx(c, j, n, -way, way).wait_recv()
        start(bx(c, j, 2, -way, way))

    def gather_first(c):
        half_in = a_dst[4 * c : 4 * c + 4].reshape(slots_n // 2, 2 * feat)
        xg[x, plane, c] = dot(squeeze((part_rows, slots_n // 2), 1), half_in).astype(BF16)
        for j in (1, 2, 3):
            start(bz(c, j, plane))
        spread_x(c, 0)

    for k in FIRST:
        start(a_copy(k, 1))
    a_pass(1)
    a_pass(2)
    for k in (1, 7, 2):
        a_copy(k, HOPS[k]).wait_recv()
    gather_first(0)
    a_pass(3)
    for j in (1, 2, 3):
        bz(0, j, order[j]).wait_recv()
        spread_x(0, j)
    relay_x(0, 0)
    for k in (6, 3, 5, 4):
        a_copy(k, HOPS[k]).wait_recv()
    gather_first(1)
    for j in (1, 2, 3):
        relay_x(0, j)
    for j in (1, 2, 3):
        bz(1, j, order[j]).wait_recv()
        spread_x(1, j)
        relay_x(1, j - 1)
    relay_x(1, 3)
    for copy in weights:
        copy.wait()
    for c in (0, 1):
        for j in range(4):
            n, way = (1, -1) if j < 2 else (0, 1)
            bx(c, j, n, -way, way).wait_recv()
            bx(c, j, 2, 2, 1).wait_recv()

    rows_n = planes * cap_rows
    half = rows_n // 2
    blocks = [xg[i].reshape(rows_n, 2 * feat) for i in range(4)]
    x_all = jnp.concatenate([b[:, :feat] for b in blocks], axis=1)
    dy_all = jnp.concatenate([b[:, feat:] for b in blocks], axis=1)
    dy_buf[...] = dy_all
    dy_copy = pltpu.make_async_copy(dy_buf, dy_hbm, out_sem.at[0])
    dy_copy.start()
    parts = (
        dot(x_all, wg[...]),
        dot(x_all, wu[...]),
        dot(dy_all, wd[...], ((1,), (1,))),
    )
    for i in range(4):
        for n, part in enumerate(parts):
            p_mine[i, :, n * 128 : (n + 1) * 128] = part[:, i * 128 : (i + 1) * 128]

    my_rows = pl.ds(pl.multiple_of(core * half, half), half)
    its_rows = pl.ds(pl.multiple_of((1 - core) * half, half), half)

    def d1(i):
        return remote(d1_src.at[i], d1_dst.at[i], d1_send.at[i], d1_recv.at[i], partner)

    wrap_y = [(y + step) % 4 for step in range(4)]
    for step in (2, 1, 3, 0):
        d1_src[step] = p_mine[wrap_y[step], its_rows, :]
        start(d1(step))

    quarter = half // 2
    top, bottom = pl.ds(0, quarter), pl.ds(quarter, quarter)

    def d2(n, way):
        return remote(d2_src.at[n], d2_dst.at[n], d2_send.at[n], d2_recv.at[n], at_y(way))

    def pair_sum(step):
        d1(step).wait_recv()
        return p_mine[wrap_y[step], my_rows, :] + d1_dst[step]

    far = pair_sum(2).astype(BF16)
    d2_src[0] = far[:quarter]
    start(d2(0, 1))
    d2_src[1] = far[quarter:]
    start(d2(1, -1))
    ahead_sum = pair_sum(1)
    d2_src[2] = ahead_sum[quarter:].astype(BF16)
    start(d2(2, 1))
    back_sum = pair_sum(3)
    d2_src[3] = back_sum[:quarter].astype(BF16)
    start(d2(3, -1))
    mine = pair_sum(0)
    d2(0, 1).wait_recv()
    d2_src[4] = (ahead_sum[:quarter] + d2_dst[0].astype(F32)).astype(BF16)
    start(d2(4, 1))
    d2(1, -1).wait_recv()
    d2_src[5] = (back_sum[quarter:] + d2_dst[1].astype(F32)).astype(BF16)
    start(d2(5, -1))
    for n, way in ((2, 1), (3, -1), (4, 1), (5, -1)):
        d2(n, way).wait_recv()
    from_back = jnp.concatenate([d2_dst[4], d2_dst[2]], axis=0).astype(F32)
    from_ahead = jnp.concatenate([d2_dst[3], d2_dst[5]], axis=0).astype(F32)
    total = mine + from_back + from_ahead

    gate, up, hidden_grad = total[:, :128], total[:, 128:256], total[:, 256:]
    sig = 1.0 / (1.0 + jnp.exp(-gate))
    hidden = (gate * sig * up).astype(BF16)
    gate_grad = (hidden_grad * up * sig * (1.0 + gate * (1.0 - sig))).astype(BF16)
    up_grad = (hidden_grad * gate * sig).astype(BF16)
    h_all[y, core] = jnp.concatenate([hidden, gate_grad, up_grad], axis=1)

    def d3_out(way):
        own = h_all.at[y, core]
        n = 0 if way == 1 else 1
        return remote(own, own, d3_send.at[n], d3_recv.at[n], at_y(way))

    def d3_in(way):
        there = h_all.at[(y - way + 4) % 4, core]
        n = 0 if way == 1 else 1
        return remote(there, there, d3_send.at[n], d3_recv.at[n], at_y(way))

    def d3_pass(way):
        n, rows = (2, top) if way == 1 else (3, bottom)
        there = h_all.at[(y - way + 4) % 4, core, rows]
        return remote(there, there, d3_send.at[n], d3_recv.at[n], at_y(way))

    def d3_far(way):
        n, rows = (2, top) if way == 1 else (3, bottom)
        there = h_all.at[(y + 2) % 4, core, rows]
        return remote(there, there, d3_send.at[n], d3_recv.at[n], at_y(way))

    def d4(step, whose):
        there = h_all.at[wrap_y[step], whose]
        return remote(there, there, d4_send.at[step], d4_recv.at[step], partner)

    start(d3_out(1))
    start(d3_out(-1))
    start(d4(0, core))
    d3_in(1).wait_recv()
    start(d3_pass(1))
    d3_in(-1).wait_recv()
    start(d3_pass(-1))
    start(d4(3, core))
    start(d4(1, core))
    d3_far(1).wait_recv()
    d3_far(-1).wait_recv()
    start(d4(2, core))
    for step in range(4):
        d4(step, 1 - core).wait_recv()

    acts = [h_all[i].reshape(rows_n, 384) for i in range(4)]
    hidden_all = jnp.concatenate([a[:, :128] for a in acts], axis=1)
    gate_grad_all = jnp.concatenate([a[:, 128:256] for a in acts], axis=1)
    up_grad_all = jnp.concatenate([a[:, 256:] for a in acts], axis=1)
    hid_buf[...] = hidden_all
    hid_copy = pltpu.make_async_copy(hid_buf, hid_hbm, out_sem.at[1])
    hid_copy.start()
    out_rows = dot(hidden_all, wd[...])
    grad_rows = dot(gate_grad_all, wg[...], ((1,), (1,))) + dot(
        up_grad_all, wu[...], ((1,), (1,))
    )
    for i in range(4):
        cols = slice(i * feat, (i + 1) * feat)
        f_mine[i] = jnp.concatenate([out_rows[:, cols], grad_rows[:, cols]], axis=1)

    mine_chunk = plane // 2
    chunks = (1 - mine_chunk, mine_chunk)

    def f(c, n, way):
        return remote(f_src.at[c, n], f_dst.at[c, n], f_send.at[c, n], f_recv.at[c, n], at_x(way))

    def f_part(c, step, lo, n):
        first = pl.multiple_of(chunks[c] * half + lo, 16)
        return f_mine[(x + step) % xs, pl.ds(first, n), :]

    for c in (0, 1):
        f_src[c, 0] = f_part(c, 2, 0, quarter).astype(BF16)
        start(f(c, 0, 1))
        f_src[c, 1] = f_part(c, 2, quarter, quarter).astype(BF16)
        start(f(c, 1, -1))
    for c in (0, 1):
        f_src[c, 2] = f_part(c, 1, quarter, quarter).astype(BF16)
        start(f(c, 2, 1))
        f_src[c, 3] = f_part(c, 3, 0, quarter).astype(BF16)
        start(f(c, 3, -1))
    for c in (0, 1):
        f(c, 0, 1).wait_recv()
        f_src[c, 4] = (f_part(c, 1, 0, quarter) + f_dst[c, 0].astype(F32)).astype(BF16)
        start(f(c, 4, 1))
        f(c, 1, -1).wait_recv()
        f_src[c, 5] = (f_part(c, 3, quarter, quarter) + f_dst[c, 1].astype(F32)).astype(BF16)
        start(f(c, 5, -1))

    def zc(j):
        return remote(z_src.at[j - 1], z_dst.at[j - 1], z_send.at[j - 1], z_recv.at[j - 1], at_plane(order[j]))

    for c in (0, 1):
        for n, way in ((2, 1), (3, -1), (4, 1), (5, -1)):
            f(c, n, way).wait_recv()
        top_sum = f_part(c, 0, 0, quarter) + f_dst[c, 4].astype(F32) + f_dst[c, 3].astype(F32)
        low_sum = f_part(c, 0, quarter, quarter) + f_dst[c, 2].astype(F32) + f_dst[c, 5].astype(F32)
        odd = plane % 2
        if c == 0:
            z_sum[0] = top_sum
            z_sum[1] = low_sum
            for j, at in ((2, odd), (3, 1 - odd)):
                z_src[j - 1] = z_sum[at].astype(BF16)
                start(zc(j))
        else:
            z_sum[2] = top_sum
            z_sum[3] = low_sum
            z_src[0] = z_sum[3 - odd].astype(BF16)
            start(zc(1))
    routes = z_sum[2 + odd]
    for j in (2, 3, 1):
        zc(j).wait_recv()
        routes = routes + z_dst[j - 1].astype(F32)

    wide = dot(squeeze((slots_n, cap_rows), 0), routes.astype(BF16))
    g_src[...] = wide.reshape(EXPERTS, SLOT, 2 * feat).astype(BF16)

    def gc(k, way):
        return remote(
            g_src.at[PLACE[k]], home_hbm.at[k], g_send.at[k - 1], g_recv.at[k - 1], at_group(way * k)
        )

    for k in (4, 3, 5, 2, 6, 1, 7):
        start(gc(k, -1))
    own_copy = pltpu.make_async_copy(g_src.at[0], home_hbm.at[0], out_sem.at[2])
    own_copy.start()
    dy_copy.wait()
    hid_copy.wait()
    own_copy.wait()
    for copy in sent:
        copy.wait_send()
    for k in range(1, 8):
        gc(k, 1).wait_recv()


def finish(home_ref, slots_ref, hid_ref, dy_ref, out_ref, grad_ref, down_hbm, down_buf, sem):
    rows, units = hid_ref.shape
    feat = out_ref.shape[1]
    step = units // 4
    copies = []
    for i in range(4):
        own = pl.ds(i * step, step)
        down_buf[own, :] = dot(hid_ref[:, own], dy_ref[...], ((0,), (0,))).astype(BF16)
        copies.append(pltpu.make_async_copy(down_buf.at[own, :], down_hbm.at[own, :], sem.at[i]))
        copies[-1].start()
    home = home_ref[...].reshape(EXPERTS * SLOT, 2 * feat).astype(F32)
    high = lax.Precision.HIGHEST
    out_ref[...] = dot(slots_ref[0], home[:, :feat], ((0,), (0,)), high).astype(BF16)
    grad_ref[...] = dot(slots_ref[1], home[:, feat:], ((0,), (0,)), high).astype(BF16)
    for copy in copies:
        copy.wait()


def per_device(tokens, cotangent, expert_ids, gate_weights, w_gate, w_up, w_down):
    tok_rows, feat = tokens.shape
    wide, units = w_gate.shape
    planes = lax.axis_size("expert") // EXPERTS
    cap_rows = EXPERTS * CAP
    rows = planes * cap_rows
    half, quarter = rows // 2, rows // 4
    vmem = pl.BlockSpec(memory_space=pltpu.VMEM)
    hbm = pl.BlockSpec(memory_space=pl.ANY)
    dma = pltpu.SemaphoreType.DMA
    block = (EXPERTS, SLOT, 2 * feat)
    part = cap_rows // 2
    home, slots, hidden, dy_rows = pl.pallas_call(
        kernel,
        out_shape=(
            jax.ShapeDtypeStruct(block, BF16),
            jax.ShapeDtypeStruct((2, EXPERTS * SLOT, tok_rows), F32),
            jax.ShapeDtypeStruct((rows, units), BF16),
            jax.ShapeDtypeStruct((rows, wide), BF16),
        ),
        in_specs=[hbm] * 7,
        out_specs=(hbm, vmem, hbm, hbm),
        scratch_shapes=[
            pltpu.VMEM((2, tok_rows), jnp.int32), pltpu.VMEM((2, tok_rows), F32),
            pltpu.VMEM((tok_rows, feat), BF16), pltpu.VMEM((tok_rows, feat), BF16), dma((4,)),
            pltpu.VMEM((wide, units), BF16), pltpu.VMEM((wide, units), BF16),
            pltpu.VMEM((units, wide), BF16), dma((3,)),
            pltpu.VMEM(block, BF16), pltpu.VMEM((len(RELAYS),) + block[1:], BF16),
            pltpu.VMEM(block, BF16), dma((len(ARRIVALS),)), dma((len(ARRIVALS),)),
            pltpu.VMEM((4, planes, 2, part, 2 * feat), BF16),
            dma((2, 3)), dma((2, 3)), dma((2, 4, 3)), dma((2, 4, 3)),
            pltpu.VMEM((4, rows, 384), F32), pltpu.VMEM((4, half, 384), F32),
            pltpu.VMEM((4, half, 384), F32), dma((4,)), dma((4,)),
            pltpu.VMEM((6, quarter, 384), BF16), pltpu.VMEM((6, quarter, 384), BF16),
            dma((6,)), dma((6,)),
            pltpu.VMEM((4, 2, half, 384), BF16), dma((4,)), dma((4,)), dma((4,)), dma((4,)),
            pltpu.VMEM((4, rows, 2 * feat), F32), pltpu.VMEM((2, 6, quarter, 2 * feat), BF16),
            pltpu.VMEM((2, 6, quarter, 2 * feat), BF16), dma((2, 6)), dma((2, 6)),
            pltpu.VMEM((4, cap_rows, 2 * feat), F32),
            pltpu.VMEM((3, cap_rows, 2 * feat), BF16), pltpu.VMEM((3, cap_rows, 2 * feat), BF16),
            dma((3,)), dma((3,)),
            pltpu.VMEM(block, BF16), dma((7,)), dma((7,)),
            pltpu.VMEM((rows, units), BF16), pltpu.VMEM((rows, wide), BF16), dma((3,)),
        ],
        compiler_params=pltpu.CompilerParams(collective_id=0, has_side_effects=True),
    )(expert_ids.T, gate_weights.T, tokens, cotangent, w_gate, w_up, w_down)
    return pl.pallas_call(
        finish,
        out_shape=(
            jax.ShapeDtypeStruct((tok_rows, feat), BF16),
            jax.ShapeDtypeStruct((tok_rows, feat), BF16),
            jax.ShapeDtypeStruct((units, wide), BF16),
        ),
        in_specs=[vmem] * 4,
        out_specs=(vmem, vmem, hbm),
        scratch_shapes=[pltpu.VMEM((units, wide), BF16), dma((4,))],
    )(home, slots, hidden, dy_rows)


def solution(mesh):
    return jax.shard_map(
        per_device,
        mesh=mesh,
        in_specs=(
            P("expert", ("dp", "tpin", "tpout")),
            P("expert", ("dp", "tpin", "tpout")),
            P("expert", None),
            P("expert", None),
            P(("dp", "tpin"), ("expert", "tpout")),
            P(("dp", "tpin"), ("expert", "tpout")),
            P(("expert", "tpout"), ("dp", "tpin")),
        ),
        out_specs=(
            P("expert", ("dp", "tpin", "tpout")),
            P("expert", ("dp", "tpin", "tpout")),
            P(("expert", "tpout"), ("dp", "tpin")),
        ),
        check_vma=False,
    )
```

```python
import jax
import jax.numpy as jnp
from jax import lax
from jax.experimental import pallas as pl
from jax.experimental.pallas import tpu as pltpu
from jax.sharding import PartitionSpec as P

EXPERTS = 8
HID = 8192
CAP = 6
SLOT = 8
MESH = pl.DeviceIdType.MESH
F32 = jnp.float32
BF16 = jnp.bfloat16

LEGS = ((), (1,), (2,), (2, 1), (0, 0), (-2, -1), (-2,), (-1,))
FIRST = (4, 3, 5, 2, 6, 1, 7)
RELAYS = (4, 3, 5)
ARRIVALS = tuple((k, h) for k in range(1, 8) for h in range(len(LEGS[k])))
PLACE = (0, 1, 3, 5, 7, 6, 4, 2)


def dot(a, b, contract=((1,), (0,)), precision=None):
    return lax.dot_general(
        a, b, (contract, ((), ())), preferred_element_type=F32, precision=precision
    )


def kernel(
    ids_hbm, gw_hbm, tok_hbm, cot_hbm, wg_hbm, wu_hbm, wd_hbm,
    home_hbm, slots_hbm, hid_hbm, dy_hbm,
    ids_ref, gw_ref, tok_ref, cot_ref, in_sem,
    wg, wu, wd, w_sem,
    a_src, a_relay, a_dst, a_send, a_recv,
    xg, b_zsend, b_zrecv, b_xsend, b_xrecv,
    p_mine, d1_src, d1_dst, d1_send, d1_recv,
    d2_src, d2_dst, d2_send, d2_recv,
    h_all, d3_send, d3_recv, d4_send, d4_recv,
    f_mine, f_src, f_dst, f_send, f_recv,
    z_sum, z_src, z_dst, z_send, z_recv,
    g_src, g_send, g_recv,
    slot_buf, hid_buf, dy_buf, out_sem,
):
    sent = []

    z = lax.axis_index("expert")
    x = lax.axis_index("tpout")
    y_hi = lax.axis_index("tpin")
    dp = lax.axis_index("dp")
    planes = lax.axis_size("expert") // EXPERTS
    group, plane = z // planes, z % planes
    core = dp % 2
    y = y_hi * 2 + dp // 2
    side = 1 - 2 * core
    xs = lax.axis_size("tpout")

    def at_group(step):
        return {"expert": ((group + step + EXPERTS) % EXPERTS) * planes + plane}

    def at_plane(p):
        return {"expert": group * planes + p}

    def at_x(step):
        return {"tpout": (x + step + xs) % xs}

    def at_y(step):
        there = (y + step + 4) % 4
        return {"tpin": there // 2, "dp": (there % 2) * 2 + core}

    partner = {"dp": dp + side}
    near_planes = (plane + 1 - 2 * (plane % 2), (plane + 2) % 4, 3 - plane)

    def remote(src, dst, send, recv, device):
        return pltpu.make_async_remote_copy(
            src_ref=src, dst_ref=dst, send_sem=send, recv_sem=recv,
            device_id=device, device_id_type=MESH,
        )

    def start(copy):
        copy.start()
        sent.append(copy)

    barrier = pltpu.get_barrier_semaphore()
    peers = [at_group(step) for step in (2, -2, 1, -1)] + [partner]
    peers += [at_plane(p) for p in near_planes]
    peers += [at(step) for at in (at_x, at_y) for step in (2, 1, 3)]
    for peer in peers:
        pl.semaphore_signal(barrier, inc=1, device_id=peer, device_id_type=MESH)
    inputs = [
        pltpu.make_async_copy(src, dst, in_sem.at[i])
        for i, (src, dst) in enumerate(
            ((ids_hbm, ids_ref), (gw_hbm, gw_ref), (tok_hbm, tok_ref), (cot_hbm, cot_ref))
        )
    ]
    for copy in inputs:
        copy.start()
    weights = [
        pltpu.make_async_copy(src, dst, w_sem.at[i])
        for i, (src, dst) in enumerate(((wg_hbm, wg), (wu_hbm, wu), (wd_hbm, wd)))
    ]
    for copy in weights:
        copy.start()
    for copy in inputs:
        copy.wait()

    ahead = (ids_ref[...] + EXPERTS - group) % EXPERTS
    gw = gw_ref[...]
    tokens_n = ahead.shape[1]
    expert_row = lax.broadcasted_iota(jnp.int32, (EXPERTS, tokens_n), 0)
    hit0 = jnp.where(expert_row == ahead[0:1, :], 1.0, 0.0).astype(F32)
    hit1 = jnp.where(expert_row == ahead[1:2, :], 1.0, 0.0).astype(F32)
    hit = hit0 + hit1
    weight = hit0 * gw[0:1, :] + hit1 * gw[1:2, :]
    before = jnp.where(
        lax.broadcasted_iota(jnp.int32, (tokens_n, tokens_n), 0)
        < lax.broadcasted_iota(jnp.int32, (tokens_n, tokens_n), 1), 1.0, 0.0
    ).astype(F32)
    rank = dot(hit, before)

    def spread(v):
        return jnp.concatenate(
            [jnp.broadcast_to(v[e : e + 1, :], (SLOT, tokens_n)) for e in range(EXPERTS)], axis=0
        )

    slots_n = EXPERTS * SLOT
    slot_j = (lax.broadcasted_iota(jnp.int32, (slots_n, tokens_n), 0) % SLOT).astype(F32)
    chosen = jnp.where(spread(rank) == slot_j, spread(hit), 0.0)
    slot_weights = chosen * spread(weight)
    chosen_b = chosen.astype(BF16)
    slot_gate = jnp.sum(slot_weights, axis=1, keepdims=True)
    x_rows = dot(chosen_b, tok_ref[...])
    dy_rows = dot(chosen_b, cot_ref[...]) * slot_gate
    feat = x_rows.shape[1]
    both = jnp.concatenate([x_rows, dy_rows], axis=1)
    a_src[...] = both.reshape(EXPERTS, SLOT, 2 * feat).astype(BF16)
    a_dst[0] = a_src[0]

    slot_buf[0] = slot_weights
    slot_buf[1] = chosen
    slot_copy = pltpu.make_async_copy(slot_buf, slots_hbm, out_sem.at[3])
    slot_copy.start()

    pl.semaphore_wait(barrier, len(peers))

    def a_copy(k, h):
        src = a_relay.at[RELAYS.index(k)] if h else a_src.at[k]
        dst = a_dst.at[PLACE[k]] if h == len(LEGS[k]) - 1 else a_relay.at[RELAYS.index(k)]
        n = ARRIVALS.index((k, h))
        return remote(src, dst, a_send.at[n], a_recv.at[n], at_group(LEGS[k][h] or 2 * side))

    def a_end(k):
        a_copy(k, len(LEGS[k]) - 1).wait_recv()

    cap_rows = EXPERTS * CAP
    part_rows = cap_rows // 2

    def squeeze(shape, long_axis):
        rows = lax.broadcasted_iota(jnp.int32, shape, long_axis)
        short = lax.broadcasted_iota(jnp.int32, shape, 1 - long_axis)
        return jnp.where(short // CAP * SLOT + short % CAP == rows, 1.0, 0.0).astype(BF16)

    order = (plane,) + near_planes

    def bz(c, j, whose):
        there = xg.at[x, whose, c]
        return remote(there, there, b_zsend.at[c, j - 1], b_zrecv.at[c, j - 1], at_plane(order[j]))

    def bx(c, j, step, whose):
        there = xg.at[whose, order[j], c]
        return remote(there, there, b_xsend.at[c, j, step - 1], b_xrecv.at[c, j, step - 1], at_x(step))

    def spread_x(c, j):
        for step in (2, 1, 3):
            start(bx(c, j, step, x))

    def gather_first(c):
        half_in = a_dst[4 * c : 4 * c + 4].reshape(slots_n // 2, 2 * feat)
        xg[x, plane, c] = dot(squeeze((part_rows, slots_n // 2), 1), half_in).astype(BF16)
        for j in (3, 2, 1):
            start(bz(c, j, plane))
        spread_x(c, 0)

    for k in FIRST:
        start(a_copy(k, 0))
    for k in RELAYS:
        a_copy(k, 0).wait_recv()
        start(a_copy(k, 1))
    for k in (1, 7, 2):
        a_end(k)
    gather_first(0)
    for j in (1, 2, 3):
        bz(0, j, order[j]).wait_recv()
        spread_x(0, j)
    for k in (6, 3, 5, 4):
        a_end(k)
    gather_first(1)
    for j in (1, 2, 3):
        bz(1, j, order[j]).wait_recv()
        spread_x(1, j)
    for copy in weights:
        copy.wait()
    for c in (0, 1):
        for j in range(4):
            for step in (1, 2, 3):
                bx(c, j, step, (x - step + xs) % xs).wait_recv()

    rows_n = planes * cap_rows
    half = rows_n // 2
    blocks = [xg[i].reshape(rows_n, 2 * feat) for i in range(4)]
    x_all = jnp.concatenate([b[:, :feat] for b in blocks], axis=1)
    dy_all = jnp.concatenate([b[:, feat:] for b in blocks], axis=1)
    dy_buf[...] = dy_all
    dy_copy = pltpu.make_async_copy(dy_buf, dy_hbm, out_sem.at[0])
    dy_copy.start()
    parts = (
        dot(x_all, wg[...]),
        dot(x_all, wu[...]),
        dot(dy_all, wd[...], ((1,), (1,))),
    )
    for i in range(4):
        for n, part in enumerate(parts):
            p_mine[i, :, n * 128 : (n + 1) * 128] = part[:, i * 128 : (i + 1) * 128]

    my_rows = pl.ds(pl.multiple_of(core * half, half), half)
    its_rows = pl.ds(pl.multiple_of((1 - core) * half, half), half)

    def d1(i):
        return remote(d1_src.at[i], d1_dst.at[i], d1_send.at[i], d1_recv.at[i], partner)

    wrap_y = [(y + step) % 4 for step in range(4)]
    for step in (2, 1, 3, 0):
        d1_src[step] = p_mine[wrap_y[step], its_rows, :]
        start(d1(step))


    def d2(step):
        return remote(
            d2_src.at[step - 1], d2_dst.at[step - 1], d2_send.at[step - 1], d2_recv.at[step - 1], at_y(step)
        )

    def pair_sum(step):
        d1(step).wait_recv()
        return p_mine[wrap_y[step], my_rows, :] + d1_dst[step]

    for step in (2, 1, 3):
        d2_src[step - 1] = pair_sum(step).astype(BF16)
        start(d2(step))
    total = pair_sum(0)
    for step in (1, 3, 2):
        d2(step).wait_recv()
        total = total + d2_dst[step - 1].astype(F32)

    gate, up, hidden_grad = total[:, :128], total[:, 128:256], total[:, 256:]
    sig = 1.0 / (1.0 + jnp.exp(-gate))
    hidden = (gate * sig * up).astype(BF16)
    gate_grad = (hidden_grad * up * sig * (1.0 + gate * (1.0 - sig))).astype(BF16)
    up_grad = (hidden_grad * gate * sig).astype(BF16)
    h_all[y, core] = jnp.concatenate([hidden, gate_grad, up_grad], axis=1)

    def d3(step, whose):
        there = h_all.at[whose, core]
        return remote(there, there, d3_send.at[step - 1], d3_recv.at[step - 1], at_y(step))

    def d4(step, whose):
        there = h_all.at[wrap_y[step], whose]
        return remote(there, there, d4_send.at[step], d4_recv.at[step], partner)

    for step in (2, 1, 3):
        start(d3(step, y))
    start(d4(0, core))
    for step in (1, 3, 2):
        d3(step, wrap_y[4 - step]).wait_recv()
        start(d4(4 - step, core))
    for step in range(4):
        d4(step, 1 - core).wait_recv()

    acts = [h_all[i].reshape(rows_n, 384) for i in range(4)]
    hidden_all = jnp.concatenate([a[:, :128] for a in acts], axis=1)
    gate_grad_all = jnp.concatenate([a[:, 128:256] for a in acts], axis=1)
    up_grad_all = jnp.concatenate([a[:, 256:] for a in acts], axis=1)
    hid_buf[...] = hidden_all
    hid_copy = pltpu.make_async_copy(hid_buf, hid_hbm, out_sem.at[1])
    hid_copy.start()
    out_rows = dot(hidden_all, wd[...])
    grad_rows = dot(gate_grad_all, wg[...], ((1,), (1,))) + dot(
        up_grad_all, wu[...], ((1,), (1,))
    )
    for i in range(4):
        cols = slice(i * feat, (i + 1) * feat)
        f_mine[i] = jnp.concatenate([out_rows[:, cols], grad_rows[:, cols]], axis=1)

    mine_chunk = plane // 2
    chunks = (1 - mine_chunk, mine_chunk)

    def f(c, step):
        n = step - 1
        return remote(f_src.at[c, n], f_dst.at[c, n], f_send.at[c, n], f_recv.at[c, n], at_x(step))

    def f_part(c, step):
        return f_mine[(x + step) % xs, pl.ds(pl.multiple_of(chunks[c] * half, half), half), :]

    for c in (0, 1):
        for step in (2, 1, 3):
            f_src[c, step - 1] = f_part(c, step).astype(BF16)
            start(f(c, step))

    def zc(j):
        return remote(z_src.at[j - 1], z_dst.at[j - 1], z_send.at[j - 1], z_recv.at[j - 1], at_plane(order[j]))

    odd = plane % 2
    for c in (0, 1):
        chunk_sum = f_part(c, 0)
        for step in (1, 3, 2):
            f(c, step).wait_recv()
            chunk_sum = chunk_sum + f_dst[c, step - 1].astype(F32)
        z_sum[2 * c] = chunk_sum[:cap_rows]
        z_sum[2 * c + 1] = chunk_sum[cap_rows:]
        for j, at in ((3, 1 - odd), (2, odd)) if c == 0 else ((1, 3 - odd),):
            z_src[j - 1] = z_sum[at].astype(BF16)
            start(zc(j))
    routes = z_sum[2 + odd]
    for j in (2, 3, 1):
        zc(j).wait_recv()
        routes = routes + z_dst[j - 1].astype(F32)

    wide = dot(squeeze((slots_n, cap_rows), 0), routes.astype(BF16))
    g_src[...] = wide.reshape(EXPERTS, SLOT, 2 * feat).astype(BF16)

    def gc(k, way):
        return remote(
            g_src.at[PLACE[k]], home_hbm.at[k], g_send.at[k - 1], g_recv.at[k - 1], at_group(way * k)
        )

    for k in (4, 3, 5, 2, 6, 1, 7):
        start(gc(k, -1))
    own_copy = pltpu.make_async_copy(g_src.at[0], home_hbm.at[0], out_sem.at[2])
    own_copy.start()
    dy_copy.wait()
    hid_copy.wait()
    own_copy.wait()
    slot_copy.wait()
    for copy in sent:
        copy.wait_send()
    for k in range(1, 8):
        gc(k, 1).wait_recv()


def finish(
    home_hbm, slots_hbm, hid_hbm, dy_hbm, out_hbm, grad_hbm, down_hbm,
    home_ref, slots_ref, hid_ref, dy_ref, out_ref, grad_ref, down_buf, in_sem, sem,
):
    rows, units = hid_ref.shape
    feat = out_ref.shape[1]
    step = units // 4
    inputs = [
        pltpu.make_async_copy(src, dst, in_sem.at[i])
        for i, (src, dst) in enumerate(
            ((hid_hbm, hid_ref), (dy_hbm, dy_ref), (home_hbm, home_ref), (slots_hbm, slots_ref))
        )
    ]
    for copy in inputs:
        copy.start()
    copies = []

    def put(src, dst):
        copies.append(pltpu.make_async_copy(src, dst, sem.at[len(copies)]))
        copies[-1].start()

    inputs[0].wait()
    inputs[1].wait()
    for i in range(4):
        own = pl.ds(i * step, step)
        down_buf[own, :] = dot(hid_ref[:, own], dy_ref[...], ((0,), (0,))).astype(BF16)
        put(down_buf.at[own, :], down_hbm.at[own, :])
    inputs[2].wait()
    inputs[3].wait()
    home = home_ref[...].reshape(EXPERTS * SLOT, 2 * feat).astype(F32)
    high = lax.Precision.HIGHEST
    out_ref[...] = dot(slots_ref[0], home[:, :feat], ((0,), (0,)), high).astype(BF16)
    put(out_ref, out_hbm)
    grad_ref[...] = dot(slots_ref[1], home[:, feat:], ((0,), (0,)), high).astype(BF16)
    put(grad_ref, grad_hbm)
    for copy in copies:
        copy.wait()


def per_device(tokens, cotangent, expert_ids, gate_weights, w_gate, w_up, w_down):
    tok_rows, feat = tokens.shape
    wide, units = w_gate.shape
    planes = lax.axis_size("expert") // EXPERTS
    cap_rows = EXPERTS * CAP
    rows = planes * cap_rows
    half = rows // 2
    hbm = pl.BlockSpec(memory_space=pl.ANY)
    dma = pltpu.SemaphoreType.DMA
    block = (EXPERTS, SLOT, 2 * feat)
    part = cap_rows // 2
    home, slots, hidden, dy_rows = pl.pallas_call(
        kernel,
        out_shape=(
            jax.ShapeDtypeStruct(block, BF16),
            jax.ShapeDtypeStruct((2, EXPERTS * SLOT, tok_rows), F32),
            jax.ShapeDtypeStruct((rows, units), BF16),
            jax.ShapeDtypeStruct((rows, wide), BF16),
        ),
        in_specs=[hbm] * 7,
        out_specs=(hbm, hbm, hbm, hbm),
        scratch_shapes=[
            pltpu.VMEM((2, tok_rows), jnp.int32), pltpu.VMEM((2, tok_rows), F32),
            pltpu.VMEM((tok_rows, feat), BF16), pltpu.VMEM((tok_rows, feat), BF16), dma((4,)),
            pltpu.VMEM((wide, units), BF16), pltpu.VMEM((wide, units), BF16),
            pltpu.VMEM((units, wide), BF16), dma((3,)),
            pltpu.VMEM(block, BF16), pltpu.VMEM((len(RELAYS),) + block[1:], BF16),
            pltpu.VMEM(block, BF16), dma((len(ARRIVALS),)), dma((len(ARRIVALS),)),
            pltpu.VMEM((4, planes, 2, part, 2 * feat), BF16),
            dma((2, 3)), dma((2, 3)), dma((2, 4, 3)), dma((2, 4, 3)),
            pltpu.VMEM((4, rows, 384), F32), pltpu.VMEM((4, half, 384), F32),
            pltpu.VMEM((4, half, 384), F32), dma((4,)), dma((4,)),
            pltpu.VMEM((3, half, 384), BF16), pltpu.VMEM((3, half, 384), BF16),
            dma((3,)), dma((3,)),
            pltpu.VMEM((4, 2, half, 384), BF16), dma((3,)), dma((3,)), dma((4,)), dma((4,)),
            pltpu.VMEM((4, rows, 2 * feat), F32), pltpu.VMEM((2, 3, half, 2 * feat), BF16),
            pltpu.VMEM((2, 3, half, 2 * feat), BF16), dma((2, 3)), dma((2, 3)),
            pltpu.VMEM((4, cap_rows, 2 * feat), F32),
            pltpu.VMEM((3, cap_rows, 2 * feat), BF16), pltpu.VMEM((3, cap_rows, 2 * feat), BF16),
            dma((3,)), dma((3,)),
            pltpu.VMEM(block, BF16), dma((7,)), dma((7,)),
            pltpu.VMEM((2, EXPERTS * SLOT, tok_rows), F32),
            pltpu.VMEM((rows, units), BF16), pltpu.VMEM((rows, wide), BF16), dma((4,)),
        ],
        compiler_params=pltpu.CompilerParams(collective_id=0, has_side_effects=True),
    )(expert_ids.T, gate_weights.T, tokens, cotangent, w_gate, w_up, w_down)
    return pl.pallas_call(
        finish,
        out_shape=(
            jax.ShapeDtypeStruct((tok_rows, feat), BF16),
            jax.ShapeDtypeStruct((tok_rows, feat), BF16),
            jax.ShapeDtypeStruct((units, wide), BF16),
        ),
        in_specs=[hbm] * 4,
        out_specs=(hbm, hbm, hbm),
        scratch_shapes=[
            pltpu.VMEM(block, BF16), pltpu.VMEM((2, EXPERTS * SLOT, tok_rows), F32),
            pltpu.VMEM((rows, units), BF16), pltpu.VMEM((rows, wide), BF16),
            pltpu.VMEM((tok_rows, feat), BF16), pltpu.VMEM((tok_rows, feat), BF16),
            pltpu.VMEM((units, wide), BF16), dma((4,)), dma((6,)),
        ],
    )(home, slots, hidden, dy_rows)


def solution(mesh):
    return jax.shard_map(
        per_device,
        mesh=mesh,
        in_specs=(
            P("expert", ("dp", "tpin", "tpout")),
            P("expert", ("dp", "tpin", "tpout")),
            P("expert", None),
            P("expert", None),
            P(("dp", "tpin"), ("expert", "tpout")),
            P(("dp", "tpin"), ("expert", "tpout")),
            P(("expert", "tpout"), ("dp", "tpin")),
        ),
        out_specs=(
            P("expert", ("dp", "tpin", "tpout")),
            P("expert", ("dp", "tpin", "tpout")),
            P(("expert", "tpout"), ("dp", "tpin")),
        ),
        check_vma=False,
    )
```

```python
import jax
import jax.numpy as jnp
from jax import lax
from jax.experimental import pallas as pl
from jax.experimental.pallas import tpu as pltpu
from jax.sharding import PartitionSpec as P

EXPERTS = 8
HID = 8192
CAP = 6
SLOT = 8
MESH = pl.DeviceIdType.MESH
F32 = jnp.float32
BF16 = jnp.bfloat16

LEGS = ((), (1,), (2,), (2, 1), (0, 0), (-2, -1), (-2,), (-1,))
FIRST = (4, 3, 5, 2, 6, 1, 7)
RELAYS = (4, 3, 5)
ARRIVALS = tuple((k, h) for k in range(1, 8) for h in range(len(LEGS[k])))
PLACE = (0, 1, 3, 5, 7, 6, 4, 2)


def dot(a, b, contract=((1,), (0,)), precision=None):
    return lax.dot_general(
        a, b, (contract, ((), ())), preferred_element_type=F32, precision=precision
    )


def kernel(
    ids_hbm, gw_hbm, tok_hbm, cot_hbm, wg_hbm, wu_hbm, wd_hbm,
    home_hbm, slots_hbm, hid_hbm, dy_hbm,
    ids_ref, gw_ref, tok_ref, cot_ref, in_sem,
    wg, wu, wd, w_sem,
    a_src, a_relay, a_dst, a_send, a_recv,
    xg, b_zsend, b_zrecv, b_xsend, b_xrecv,
    p_mine, d1_dst, d1_send, d1_recv,
    d2_own, d2_src, d2_dst, d2_send, d2_recv,
    h_all, d3_send, d3_recv, d4_send, d4_recv,
    f_mine, f_src, f_dst, f_send, f_recv,
    z_sum, z_src, z_dst, z_send, z_recv,
    g_src, g_send, g_recv,
    slot_buf, hid_buf, dy_buf, out_sem,
):
    sent, kept = [], []

    z = lax.axis_index("expert")
    x = lax.axis_index("tpout")
    y_hi = lax.axis_index("tpin")
    dp = lax.axis_index("dp")
    planes = lax.axis_size("expert") // EXPERTS
    group, plane = z // planes, z % planes
    core = dp % 2
    y = y_hi * 2 + dp // 2
    side = 1 - 2 * core
    xs = lax.axis_size("tpout")

    def at_group(step):
        return {"expert": ((group + step + EXPERTS) % EXPERTS) * planes + plane}

    def at_plane(p):
        return {"expert": group * planes + p}

    def at_x(step):
        return {"tpout": (x + step + xs) % xs}

    def at_y(step):
        there = (y + step + 4) % 4
        return {"tpin": there // 2, "dp": (there % 2) * 2 + core}

    partner = {"dp": dp + side}
    near_planes = (plane + 1 - 2 * (plane % 2), (plane + 2) % 4, 3 - plane)

    def remote(src, dst, send, recv, device):
        return pltpu.make_async_remote_copy(
            src_ref=src, dst_ref=dst, send_sem=send, recv_sem=recv,
            device_id=device, device_id_type=MESH,
        )

    def start(copy):
        copy.start()
        sent.append(copy)

    def local(src, dst, sem):
        kept.append(pltpu.make_async_copy(src, dst, sem))
        kept[-1].start()

    barrier = pltpu.get_barrier_semaphore()
    peers = [at_group(step) for step in (2, -2, 1, -1)] + [partner]
    peers += [at_plane(p) for p in near_planes]
    peers += [at(step) for at in (at_x, at_y) for step in (2, 1, 3)]
    for peer in peers:
        pl.semaphore_signal(barrier, inc=1, device_id=peer, device_id_type=MESH)
    inputs = [
        pltpu.make_async_copy(src, dst, in_sem.at[i])
        for i, (src, dst) in enumerate(
            ((ids_hbm, ids_ref), (gw_hbm, gw_ref), (tok_hbm, tok_ref), (cot_hbm, cot_ref))
        )
    ]
    for copy in inputs:
        copy.start()
    weights = [
        pltpu.make_async_copy(src, dst, w_sem.at[i])
        for i, (src, dst) in enumerate(((wg_hbm, wg), (wu_hbm, wu), (wd_hbm, wd)))
    ]
    for copy in weights:
        copy.start()
    for copy in inputs:
        copy.wait()

    ahead = (ids_ref[...] + EXPERTS - group) % EXPERTS
    gw = gw_ref[...]
    tokens_n = ahead.shape[1]
    expert_row = lax.broadcasted_iota(jnp.int32, (EXPERTS, tokens_n), 0)
    hit0 = jnp.where(expert_row == ahead[0:1, :], 1.0, 0.0).astype(F32)
    hit1 = jnp.where(expert_row == ahead[1:2, :], 1.0, 0.0).astype(F32)
    hit = hit0 + hit1
    weight = hit0 * gw[0:1, :] + hit1 * gw[1:2, :]
    before = jnp.where(
        lax.broadcasted_iota(jnp.int32, (tokens_n, tokens_n), 0)
        < lax.broadcasted_iota(jnp.int32, (tokens_n, tokens_n), 1), 1.0, 0.0
    ).astype(F32)
    rank = dot(hit, before)

    def spread(v):
        return jnp.concatenate(
            [jnp.broadcast_to(v[e : e + 1, :], (SLOT, tokens_n)) for e in range(EXPERTS)], axis=0
        )

    slots_n = EXPERTS * SLOT
    slot_j = (lax.broadcasted_iota(jnp.int32, (slots_n, tokens_n), 0) % SLOT).astype(F32)
    chosen = jnp.where(spread(rank) == slot_j, spread(hit), 0.0)
    slot_weights = chosen * spread(weight)
    chosen_b = chosen.astype(BF16)
    slot_gate = jnp.sum(slot_weights, axis=1, keepdims=True)
    x_rows = dot(chosen_b, tok_ref[...])
    dy_rows = dot(chosen_b, cot_ref[...]) * slot_gate
    feat = x_rows.shape[1]
    both = jnp.concatenate([x_rows, dy_rows], axis=1)
    a_src[...] = both.reshape(EXPERTS, SLOT, 2 * feat).astype(BF16)
    a_dst[0] = a_src[0]

    slot_buf[0] = slot_weights
    slot_buf[1] = chosen
    local(slot_buf, slots_hbm, out_sem.at[5])

    pl.semaphore_wait(barrier, len(peers))

    def a_copy(k, h):
        src = a_relay.at[RELAYS.index(k)] if h else a_src.at[k]
        dst = a_dst.at[PLACE[k]] if h == len(LEGS[k]) - 1 else a_relay.at[RELAYS.index(k)]
        n = ARRIVALS.index((k, h))
        return remote(src, dst, a_send.at[n], a_recv.at[n], at_group(LEGS[k][h] or 2 * side))

    def a_end(k):
        a_copy(k, len(LEGS[k]) - 1).wait_recv()

    cap_rows = EXPERTS * CAP
    part_rows = cap_rows // 2

    def squeeze(shape, long_axis):
        rows = lax.broadcasted_iota(jnp.int32, shape, long_axis)
        short = lax.broadcasted_iota(jnp.int32, shape, 1 - long_axis)
        return jnp.where(short // CAP * SLOT + short % CAP == rows, 1.0, 0.0).astype(BF16)

    order = (plane,) + near_planes

    def bz(c, j, whose):
        there = xg.at[x, c, whose]
        return remote(there, there, b_zsend.at[c, j - 1], b_zrecv.at[c, j - 1], at_plane(order[j]))

    def bx(c, j, step, whose):
        there = xg.at[whose, c, order[j]]
        return remote(there, there, b_xsend.at[c, j, step - 1], b_xrecv.at[c, j, step - 1], at_x(step))

    def spread_x(c, j):
        for step in (2, 1, 3):
            start(bx(c, j, step, x))

    def gather(c):
        half_in = a_dst[4 * c : 4 * c + 4].reshape(slots_n // 2, 2 * feat)
        xg[x, c, plane] = dot(squeeze((part_rows, slots_n // 2), 1), half_in).astype(BF16)
        for j in (3, 2, 1):
            start(bz(c, j, plane))
        spread_x(c, 0)

    def gather_x(c):
        for j in (1, 2, 3):
            bz(c, j, order[j]).wait_recv()
            spread_x(c, j)

    half = planes * part_rows
    core_rows = half // 2
    my_rows = pl.ds(pl.multiple_of(core * core_rows, core_rows), core_rows)
    its_rows = pl.ds(pl.multiple_of((1 - core) * core_rows, core_rows), core_rows)
    wrap_y = [(y + step) % 4 for step in range(4)]

    def d1(c, i):
        return remote(
            p_mine.at[c, wrap_y[i], its_rows], d1_dst.at[c, i], d1_send.at[c, i], d1_recv.at[c, i], partner
        )

    def products(c):
        for j in range(4):
            for step in (1, 2, 3):
                bx(c, j, step, (x - step + xs) % xs).wait_recv()
        blocks = [xg[i, c].reshape(half, 2 * feat) for i in range(4)]
        x_all = jnp.concatenate([b[:, :feat] for b in blocks], axis=1)
        dy_all = jnp.concatenate([b[:, feat:] for b in blocks], axis=1)
        parts = (
            dot(x_all, wg[...]),
            dot(x_all, wu[...]),
            dot(dy_all, wd[...], ((1,), (1,))),
        )
        for i in range(4):
            for n, part in enumerate(parts):
                p_mine[c, i, :, n * 128 : (n + 1) * 128] = part[:, i * 128 : (i + 1) * 128]
        for step in (2, 1, 3, 0):
            start(d1(c, step))
        rows = pl.ds(c * half, half)
        dy_buf[rows, :] = dy_all
        local(dy_buf.at[rows], dy_hbm.at[rows], out_sem.at[c])

    def d2(c, step):
        n = step - 1
        return remote(d2_src.at[c, n], d2_dst.at[c, n], d2_send.at[c, n], d2_recv.at[c, n], at_y(step))

    def pair_sum(c, step):
        d1(c, step).wait_recv()
        return p_mine[c, wrap_y[step], my_rows, :] + d1_dst[c, step]

    def sum_cores(c):
        for step in (2, 1, 3):
            d2_src[c, step - 1] = pair_sum(c, step).astype(BF16)
            start(d2(c, step))
        d2_own[c] = pair_sum(c, 0)

    def d3(c, step, whose):
        there = h_all.at[c, whose, core]
        return remote(there, there, d3_send.at[c, step - 1], d3_recv.at[c, step - 1], at_y(step))

    def d4(c, step, whose):
        there = h_all.at[c, wrap_y[step], whose]
        return remote(there, there, d4_send.at[c, step], d4_recv.at[c, step], partner)

    def activate(c):
        total = d2_own[c]
        for step in (1, 3, 2):
            d2(c, step).wait_recv()
            total = total + d2_dst[c, step - 1].astype(F32)
        gate, up, hidden_grad = total[:, :128], total[:, 128:256], total[:, 256:]
        sig = 1.0 / (1.0 + jnp.exp(-gate))
        hidden = (gate * sig * up).astype(BF16)
        gate_grad = (hidden_grad * up * sig * (1.0 + gate * (1.0 - sig))).astype(BF16)
        up_grad = (hidden_grad * gate * sig).astype(BF16)
        h_all[c, y, core] = jnp.concatenate([hidden, gate_grad, up_grad], axis=1)
        for step in (2, 1, 3):
            start(d3(c, step, y))
        start(d4(c, 0, core))

    def spread_core(c):
        for step in (1, 3, 2):
            d3(c, step, wrap_y[4 - step]).wait_recv()
            start(d4(c, 4 - step, core))

    def f(c, step):
        n = step - 1
        return remote(f_src.at[c, n], f_dst.at[c, n], f_send.at[c, n], f_recv.at[c, n], at_x(step))

    def results(c):
        for step in range(4):
            d4(c, step, 1 - core).wait_recv()
        acts = [h_all[c, i].reshape(half, 384) for i in range(4)]
        hidden_all = jnp.concatenate([a[:, :128] for a in acts], axis=1)
        gate_grad_all = jnp.concatenate([a[:, 128:256] for a in acts], axis=1)
        up_grad_all = jnp.concatenate([a[:, 256:] for a in acts], axis=1)
        out_rows = dot(hidden_all, wd[...])
        grad_rows = dot(gate_grad_all, wg[...], ((1,), (1,))) + dot(
            up_grad_all, wu[...], ((1,), (1,))
        )
        for i in range(4):
            cols = slice(i * feat, (i + 1) * feat)
            f_mine[c, i] = jnp.concatenate([out_rows[:, cols], grad_rows[:, cols]], axis=1)
        for step in (2, 1, 3):
            f_src[c, step - 1] = f_mine[c, (x + step) % xs].astype(BF16)
            start(f(c, step))
        rows = pl.ds(c * half, half)
        hid_buf[rows, :] = hidden_all
        local(hid_buf.at[rows], hid_hbm.at[rows], out_sem.at[2 + c])

    def zc(c, j):
        n = j - 1
        return remote(z_src.at[c, n], z_dst.at[c, n], z_send.at[c, n], z_recv.at[c, n], at_plane(order[j]))

    def sum_x(c):
        chunk_sum = f_mine[c, x]
        for step in (1, 3, 2):
            f(c, step).wait_recv()
            chunk_sum = chunk_sum + f_dst[c, step - 1].astype(F32)
        z_sum[c] = chunk_sum.reshape(planes, part_rows, 2 * feat)
        for j in (3, 2, 1):
            z_src[c, j - 1] = z_sum[c, order[j]].astype(BF16)
            start(zc(c, j))

    def gc(k, way):
        return remote(
            g_src.at[PLACE[k]], home_hbm.at[k], g_send.at[k - 1], g_recv.at[k - 1], at_group(way * k)
        )

    def go_home(c):
        routes = z_sum[c, plane]
        for j in (1, 2, 3):
            zc(c, j).wait_recv()
            routes = routes + z_dst[c, j - 1].astype(F32)
        wide = dot(squeeze((slots_n // 2, part_rows), 0), routes.astype(BF16))
        g_src[4 * c : 4 * c + 4] = wide.reshape(EXPERTS // 2, SLOT, 2 * feat).astype(BF16)
        for k in (4, 3, 5, 6) if c else (2, 1, 7):
            start(gc(k, -1))

    for k in FIRST:
        start(a_copy(k, 0))
    for k in RELAYS:
        a_copy(k, 0).wait_recv()
        start(a_copy(k, 1))
    for k in (1, 7, 2):
        a_end(k)
    gather(0)
    gather_x(0)
    for k in (6, 3, 5, 4):
        a_end(k)
    gather(1)
    for copy in weights:
        copy.wait()
    products(0)
    sum_cores(0)
    gather_x(1)
    activate(0)
    products(1)
    sum_cores(1)
    spread_core(0)
    results(0)
    activate(1)
    sum_x(0)
    spread_core(1)
    results(1)
    go_home(0)
    local(g_src.at[0], home_hbm.at[0], out_sem.at[4])
    sum_x(1)
    go_home(1)
    for copy in kept:
        copy.wait()
    for copy in sent:
        copy.wait_send()
    for k in range(1, 8):
        gc(k, 1).wait_recv()


def finish(
    home_hbm, slots_hbm, hid_hbm, dy_hbm, out_hbm, grad_hbm, down_hbm,
    home_ref, slots_ref, hid_ref, dy_ref, out_ref, grad_ref, down_buf, in_sem, sem,
):
    rows, units = hid_ref.shape
    feat = out_ref.shape[1]
    step = units // 4
    inputs = [
        pltpu.make_async_copy(src, dst, in_sem.at[i])
        for i, (src, dst) in enumerate(
            ((hid_hbm, hid_ref), (dy_hbm, dy_ref), (home_hbm, home_ref), (slots_hbm, slots_ref))
        )
    ]
    for copy in inputs:
        copy.start()
    copies = []

    def put(src, dst):
        copies.append(pltpu.make_async_copy(src, dst, sem.at[len(copies)]))
        copies[-1].start()

    inputs[0].wait()
    inputs[1].wait()
    for i in range(4):
        own = pl.ds(i * step, step)
        down_buf[own, :] = dot(hid_ref[:, own], dy_ref[...], ((0,), (0,))).astype(BF16)
        put(down_buf.at[own, :], down_hbm.at[own, :])
    inputs[2].wait()
    inputs[3].wait()
    home = home_ref[...].reshape(EXPERTS * SLOT, 2 * feat).astype(F32)
    high = lax.Precision.HIGHEST
    out_ref[...] = dot(slots_ref[0], home[:, :feat], ((0,), (0,)), high).astype(BF16)
    put(out_ref, out_hbm)
    grad_ref[...] = dot(slots_ref[1], home[:, feat:], ((0,), (0,)), high).astype(BF16)
    put(grad_ref, grad_hbm)
    for copy in copies:
        copy.wait()


def per_device(tokens, cotangent, expert_ids, gate_weights, w_gate, w_up, w_down):
    tok_rows, feat = tokens.shape
    wide, units = w_gate.shape
    planes = lax.axis_size("expert") // EXPERTS
    cap_rows = EXPERTS * CAP
    rows = planes * cap_rows
    half = rows // 2
    hbm = pl.BlockSpec(memory_space=pl.ANY)
    dma = pltpu.SemaphoreType.DMA
    block = (EXPERTS, SLOT, 2 * feat)
    part = cap_rows // 2
    home, slots, hidden, dy_rows = pl.pallas_call(
        kernel,
        out_shape=(
            jax.ShapeDtypeStruct(block, BF16),
            jax.ShapeDtypeStruct((2, EXPERTS * SLOT, tok_rows), F32),
            jax.ShapeDtypeStruct((rows, units), BF16),
            jax.ShapeDtypeStruct((rows, wide), BF16),
        ),
        in_specs=[hbm] * 7,
        out_specs=(hbm, hbm, hbm, hbm),
        scratch_shapes=[
            pltpu.VMEM((2, tok_rows), jnp.int32), pltpu.VMEM((2, tok_rows), F32),
            pltpu.VMEM((tok_rows, feat), BF16), pltpu.VMEM((tok_rows, feat), BF16), dma((4,)),
            pltpu.VMEM((wide, units), BF16), pltpu.VMEM((wide, units), BF16),
            pltpu.VMEM((units, wide), BF16), dma((3,)),
            pltpu.VMEM(block, BF16), pltpu.VMEM((len(RELAYS),) + block[1:], BF16),
            pltpu.VMEM(block, BF16), dma((len(ARRIVALS),)), dma((len(ARRIVALS),)),
            pltpu.VMEM((4, 2, planes, part, 2 * feat), BF16),
            dma((2, 3)), dma((2, 3)), dma((2, 4, 3)), dma((2, 4, 3)),
            pltpu.VMEM((2, 4, half, 384), F32), pltpu.VMEM((2, 4, half // 2, 384), F32), dma((2, 4)), dma((2, 4)),
            pltpu.VMEM((2, half // 2, 384), F32),
            pltpu.VMEM((2, 3, half // 2, 384), BF16), pltpu.VMEM((2, 3, half // 2, 384), BF16),
            dma((2, 3)), dma((2, 3)),
            pltpu.VMEM((2, 4, 2, half // 2, 384), BF16), dma((2, 3)), dma((2, 3)), dma((2, 4)), dma((2, 4)),
            pltpu.VMEM((2, 4, half, 2 * feat), F32), pltpu.VMEM((2, 3, half, 2 * feat), BF16),
            pltpu.VMEM((2, 3, half, 2 * feat), BF16), dma((2, 3)), dma((2, 3)),
            pltpu.VMEM((2, planes, part, 2 * feat), F32),
            pltpu.VMEM((2, 3, part, 2 * feat), BF16), pltpu.VMEM((2, 3, part, 2 * feat), BF16),
            dma((2, 3)), dma((2, 3)),
            pltpu.VMEM(block, BF16), dma((7,)), dma((7,)),
            pltpu.VMEM((2, EXPERTS * SLOT, tok_rows), F32),
            pltpu.VMEM((rows, units), BF16), pltpu.VMEM((rows, wide), BF16), dma((6,)),
        ],
        compiler_params=pltpu.CompilerParams(collective_id=0, has_side_effects=True),
    )(expert_ids.T, gate_weights.T, tokens, cotangent, w_gate, w_up, w_down)
    return pl.pallas_call(
        finish,
        out_shape=(
            jax.ShapeDtypeStruct((tok_rows, feat), BF16),
            jax.ShapeDtypeStruct((tok_rows, feat), BF16),
            jax.ShapeDtypeStruct((units, wide), BF16),
        ),
        in_specs=[hbm] * 4,
        out_specs=(hbm, hbm, hbm),
        scratch_shapes=[
            pltpu.VMEM(block, BF16), pltpu.VMEM((2, EXPERTS * SLOT, tok_rows), F32),
            pltpu.VMEM((rows, units), BF16), pltpu.VMEM((rows, wide), BF16),
            pltpu.VMEM((tok_rows, feat), BF16), pltpu.VMEM((tok_rows, feat), BF16),
            pltpu.VMEM((units, wide), BF16), dma((4,)), dma((6,)),
        ],
    )(home, slots, hidden, dy_rows)


def solution(mesh):
    return jax.shard_map(
        per_device,
        mesh=mesh,
        in_specs=(
            P("expert", ("dp", "tpin", "tpout")),
            P("expert", ("dp", "tpin", "tpout")),
            P("expert", None),
            P("expert", None),
            P(("dp", "tpin"), ("expert", "tpout")),
            P(("dp", "tpin"), ("expert", "tpout")),
            P(("expert", "tpout"), ("dp", "tpin")),
        ),
        out_specs=(
            P("expert", ("dp", "tpin", "tpout")),
            P("expert", ("dp", "tpin", "tpout")),
            P(("expert", "tpout"), ("dp", "tpin")),
        ),
        check_vma=False,
    )
```

```python
import jax
import jax.numpy as jnp
from jax import lax
from jax.experimental import pallas as pl
from jax.experimental.pallas import tpu as pltpu
from jax.sharding import PartitionSpec as P

EXPERTS = 8
HID = 8192
CAP = 6
SLOT = 8
MESH = pl.DeviceIdType.MESH
F32 = jnp.float32
BF16 = jnp.bfloat16

LEGS = ((), (1,), (2,), (2, 1), (0, 0), (-2, -1), (-2,), (-1,))
FIRST = (4, 3, 5, 2, 6, 1, 7)
RELAYS = (4, 3, 5)
ARRIVALS = tuple((k, h) for k in range(1, 8) for h in range(len(LEGS[k])))
PLACE = (0, 1, 3, 5, 7, 6, 4, 2)


def dot(a, b, contract=((1,), (0,)), precision=None):
    return lax.dot_general(
        a, b, (contract, ((), ())), preferred_element_type=F32, precision=precision
    )


def kernel(
    ids_hbm, gw_hbm, tok_hbm, cot_hbm, wg_hbm, wu_hbm, wd_hbm,
    home_hbm, slots_hbm, hid_hbm, dy_hbm,
    ids_ref, gw_ref, tok_ref, cot_ref, in_sem,
    wg, wu, wd, w_sem,
    a_src, a_relay, a_dst, a_send, a_recv,
    xg, b_zsend, b_zrecv, b_xsend, b_xrecv,
    p_mine, d1_dst, d1_send, d1_recv,
    d2_own, d2_src, d2_dst, d2_send, d2_recv,
    h_all, d3_send, d3_recv, d4_send, d4_recv,
    f_mine, f_src, f_dst, f_send, f_recv,
    z_sum, z_src, z_dst, z_send, z_recv,
    g_src, g_send, g_recv,
    slot_buf, hid_buf, dy_buf, out_sem,
):
    sent, kept = [], []

    z = lax.axis_index("expert")
    x = lax.axis_index("tpout")
    y_hi = lax.axis_index("tpin")
    dp = lax.axis_index("dp")
    planes = lax.axis_size("expert") // EXPERTS
    group, plane = z // planes, z % planes
    core = dp % 2
    y = y_hi * 2 + dp // 2
    side = 1 - 2 * core
    xs = lax.axis_size("tpout")

    def at_group(step):
        return {"expert": ((group + step + EXPERTS) % EXPERTS) * planes + plane}

    def at_plane(p):
        return {"expert": group * planes + p}

    def at_x(step):
        return {"tpout": (x + step + xs) % xs}

    def at_y(step):
        there = (y + step + 4) % 4
        return {"tpin": there // 2, "dp": (there % 2) * 2 + core}

    partner = {"dp": dp + side}
    near_planes = (plane + 1 - 2 * (plane % 2), (plane + 2) % 4, 3 - plane)

    def remote(src, dst, send, recv, device):
        return pltpu.make_async_remote_copy(
            src_ref=src, dst_ref=dst, send_sem=send, recv_sem=recv,
            device_id=device, device_id_type=MESH,
        )

    def start(copy):
        copy.start()
        sent.append(copy)

    def local(src, dst, sem):
        kept.append(pltpu.make_async_copy(src, dst, sem))
        kept[-1].start()

    barrier = pltpu.get_barrier_semaphore()
    peers = [at_group(step) for step in (2, -2, 1, -1)] + [partner]
    peers += [at_plane(p) for p in near_planes]
    peers += [at(step) for at in (at_x, at_y) for step in (2, 1, 3)]
    for peer in peers:
        pl.semaphore_signal(barrier, inc=1, device_id=peer, device_id_type=MESH)
    inputs = [
        pltpu.make_async_copy(src, dst, in_sem.at[i])
        for i, (src, dst) in enumerate(
            ((ids_hbm, ids_ref), (gw_hbm, gw_ref), (tok_hbm, tok_ref), (cot_hbm, cot_ref))
        )
    ]
    for copy in inputs:
        copy.start()
    weights = [
        pltpu.make_async_copy(src, dst, w_sem.at[i])
        for i, (src, dst) in enumerate(((wg_hbm, wg), (wu_hbm, wu), (wd_hbm, wd)))
    ]
    for copy in weights:
        copy.start()
    for copy in inputs:
        copy.wait()

    ahead = (ids_ref[...] + EXPERTS - group) % EXPERTS
    gw = gw_ref[...]
    tokens_n = ahead.shape[1]
    expert_row = lax.broadcasted_iota(jnp.int32, (EXPERTS, tokens_n), 0)
    hit0 = jnp.where(expert_row == ahead[0:1, :], 1.0, 0.0).astype(F32)
    hit1 = jnp.where(expert_row == ahead[1:2, :], 1.0, 0.0).astype(F32)
    hit = hit0 + hit1
    weight = hit0 * gw[0:1, :] + hit1 * gw[1:2, :]
    before = jnp.where(
        lax.broadcasted_iota(jnp.int32, (tokens_n, tokens_n), 0)
        < lax.broadcasted_iota(jnp.int32, (tokens_n, tokens_n), 1), 1.0, 0.0
    ).astype(F32)
    rank = dot(hit, before)

    def spread(v):
        return jnp.concatenate(
            [jnp.broadcast_to(v[e : e + 1, :], (SLOT, tokens_n)) for e in range(EXPERTS)], axis=0
        )

    slots_n = EXPERTS * SLOT
    slot_j = (lax.broadcasted_iota(jnp.int32, (slots_n, tokens_n), 0) % SLOT).astype(F32)
    chosen = jnp.where(spread(rank) == slot_j, spread(hit), 0.0)
    slot_weights = chosen * spread(weight)
    chosen_b = chosen.astype(BF16)
    slot_gate = jnp.sum(slot_weights, axis=1, keepdims=True)
    x_rows = dot(chosen_b, tok_ref[...])
    dy_rows = dot(chosen_b, cot_ref[...]) * slot_gate
    feat = x_rows.shape[1]
    both = jnp.concatenate([x_rows, dy_rows], axis=1)
    a_src[...] = both.reshape(EXPERTS, SLOT, 2 * feat).astype(BF16)
    a_dst[0] = a_src[0]

    slot_buf[0] = slot_weights
    slot_buf[1] = chosen
    local(slot_buf, slots_hbm, out_sem.at[5])

    pl.semaphore_wait(barrier, len(peers))

    def a_copy(k, h):
        src = a_relay.at[RELAYS.index(k)] if h else a_src.at[k]
        dst = a_dst.at[PLACE[k]] if h == len(LEGS[k]) - 1 else a_relay.at[RELAYS.index(k)]
        n = ARRIVALS.index((k, h))
        return remote(src, dst, a_send.at[n], a_recv.at[n], at_group(LEGS[k][h] or 2 * side))

    def a_end(k):
        a_copy(k, len(LEGS[k]) - 1).wait_recv()

    cap_rows = EXPERTS * CAP
    part_rows = cap_rows // 2

    def squeeze(shape, long_axis):
        rows = lax.broadcasted_iota(jnp.int32, shape, long_axis)
        short = lax.broadcasted_iota(jnp.int32, shape, 1 - long_axis)
        return jnp.where(short // CAP * SLOT + short % CAP == rows, 1.0, 0.0).astype(BF16)

    order = (plane,) + near_planes

    def bz(c, j, whose):
        there = xg.at[x, c, whose]
        return remote(there, there, b_zsend.at[c, j - 1], b_zrecv.at[c, j - 1], at_plane(order[j]))

    def bx(c, j, step, whose):
        there = xg.at[whose, c, order[j]]
        return remote(there, there, b_xsend.at[c, j, step - 1], b_xrecv.at[c, j, step - 1], at_x(step))

    def spread_x(c, j):
        for step in (2, 1, 3):
            start(bx(c, j, step, x))

    def gather(c):
        half_in = a_dst[4 * c : 4 * c + 4].reshape(slots_n // 2, 2 * feat)
        xg[x, c, plane] = dot(squeeze((part_rows, slots_n // 2), 1), half_in).astype(BF16)
        for j in (3, 2, 1):
            start(bz(c, j, plane))
        spread_x(c, 0)

    def gather_x(c):
        for j in (1, 2, 3):
            bz(c, j, order[j]).wait_recv()
            spread_x(c, j)

    half = planes * part_rows
    core_rows = half // 2
    my_rows = pl.ds(pl.multiple_of(core * core_rows, core_rows), core_rows)
    its_rows = pl.ds(pl.multiple_of((1 - core) * core_rows, core_rows), core_rows)
    wrap_y = [(y + step) % 4 for step in range(4)]

    def d1(c, i):
        return remote(
            p_mine.at[c, wrap_y[i], its_rows], d1_dst.at[c, i], d1_send.at[c, i], d1_recv.at[c, i], partner
        )

    def products(c):
        for j in range(4):
            for step in (1, 2, 3):
                bx(c, j, step, (x - step + xs) % xs).wait_recv()
        blocks = [xg[i, c].reshape(half, 2 * feat) for i in range(4)]
        x_all = jnp.concatenate([b[:, :feat] for b in blocks], axis=1)
        dy_all = jnp.concatenate([b[:, feat:] for b in blocks], axis=1)
        parts = (
            dot(x_all, wg[...]),
            dot(x_all, wu[...]),
            dot(dy_all, wd[...], ((1,), (1,))),
        )
        for i in range(4):
            for n, part in enumerate(parts):
                p_mine[c, i, :, n * 128 : (n + 1) * 128] = part[:, i * 128 : (i + 1) * 128]
        for step in (2, 1, 3, 0):
            start(d1(c, step))
        rows = pl.ds(c * half, half)
        dy_buf[rows, :] = dy_all
        local(dy_buf.at[rows], dy_hbm.at[rows], out_sem.at[c])

    def d2(c, step):
        n = step - 1
        return remote(d2_src.at[c, n], d2_dst.at[c, n], d2_send.at[c, n], d2_recv.at[c, n], at_y(step))

    def pair_sum(c, step):
        d1(c, step).wait_recv()
        return p_mine[c, wrap_y[step], my_rows, :] + d1_dst[c, step]

    def sum_cores(c):
        for step in (2, 1, 3):
            d2_src[c, step - 1] = pair_sum(c, step).astype(BF16)
            start(d2(c, step))
        d2_own[c] = pair_sum(c, 0)

    def d3(c, step, whose):
        there = h_all.at[c, whose, core]
        return remote(there, there, d3_send.at[c, step - 1], d3_recv.at[c, step - 1], at_y(step))

    def d4(c, step, whose):
        there = h_all.at[c, wrap_y[step], whose]
        return remote(there, there, d4_send.at[c, step], d4_recv.at[c, step], partner)

    def activate(c):
        total = d2_own[c]
        for step in (1, 3, 2):
            d2(c, step).wait_recv()
            total = total + d2_dst[c, step - 1].astype(F32)
        gate, up, hidden_grad = total[:, :128], total[:, 128:256], total[:, 256:]
        sig = 1.0 / (1.0 + jnp.exp(-gate))
        hidden = (gate * sig * up).astype(BF16)
        gate_grad = (hidden_grad * up * sig * (1.0 + gate * (1.0 - sig))).astype(BF16)
        up_grad = (hidden_grad * gate * sig).astype(BF16)
        h_all[c, y, core] = jnp.concatenate([hidden, gate_grad, up_grad], axis=1)
        for step in (2, 1, 3):
            start(d3(c, step, y))
        start(d4(c, 0, core))

    def spread_core(c):
        for step in (1, 3, 2):
            d3(c, step, wrap_y[4 - step]).wait_recv()
            start(d4(c, 4 - step, core))

    def f(c, step):
        n = step - 1
        return remote(f_src.at[c, n], f_dst.at[c, n], f_send.at[c, n], f_recv.at[c, n], at_x(step))

    def results(c):
        for step in range(4):
            d4(c, step, 1 - core).wait_recv()
        acts = [h_all[c, i].reshape(half, 384) for i in range(4)]
        hidden_all = jnp.concatenate([a[:, :128] for a in acts], axis=1)
        gate_grad_all = jnp.concatenate([a[:, 128:256] for a in acts], axis=1)
        up_grad_all = jnp.concatenate([a[:, 256:] for a in acts], axis=1)
        out_rows = dot(hidden_all, wd[...])
        grad_rows = dot(gate_grad_all, wg[...], ((1,), (1,))) + dot(
            up_grad_all, wu[...], ((1,), (1,))
        )
        for i in range(4):
            cols = slice(i * feat, (i + 1) * feat)
            f_mine[c, i] = jnp.concatenate([out_rows[:, cols], grad_rows[:, cols]], axis=1)
        for step in (2, 1, 3):
            f_src[c, step - 1] = f_mine[c, (x + step) % xs].astype(BF16)
            start(f(c, step))
        rows = pl.ds(c * half, half)
        hid_buf[rows, :] = hidden_all
        local(hid_buf.at[rows], hid_hbm.at[rows], out_sem.at[2 + c])

    def zc(c, j):
        n = j - 1
        return remote(z_src.at[c, n], z_dst.at[c, n], z_send.at[c, n], z_recv.at[c, n], at_plane(order[j]))

    def sum_x(c):
        chunk_sum = f_mine[c, x]
        for step in (1, 3, 2):
            f(c, step).wait_recv()
            chunk_sum = chunk_sum + f_dst[c, step - 1].astype(F32)
        z_sum[c] = chunk_sum.reshape(planes, part_rows, 2 * feat)
        for j in (3, 2, 1):
            z_src[c, j - 1] = z_sum[c, order[j]].astype(BF16)
            start(zc(c, j))

    def gc(k, way):
        return remote(
            g_src.at[PLACE[k]], home_hbm.at[k], g_send.at[k - 1], g_recv.at[k - 1], at_group(way * k)
        )

    def go_home(c):
        routes = z_sum[c, plane]
        for j in (1, 2, 3):
            zc(c, j).wait_recv()
            routes = routes + z_dst[c, j - 1].astype(F32)
        wide = dot(squeeze((slots_n // 2, part_rows), 0), routes.astype(BF16))
        g_src[4 * c : 4 * c + 4] = wide.reshape(EXPERTS // 2, SLOT, 2 * feat).astype(BF16)
        for k in (4, 3, 5, 6) if c else (2, 1, 7):
            start(gc(k, -1))

    for k in FIRST:
        start(a_copy(k, 0))
    for k in RELAYS:
        a_copy(k, 0).wait_recv()
        start(a_copy(k, 1))
    for k in (1, 7, 2):
        a_end(k)
    gather(0)
    gather_x(0)
    for k in (6, 3, 5, 4):
        a_end(k)
    gather(1)
    for copy in weights:
        copy.wait()
    products(0)
    gather_x(1)
    sum_cores(0)
    products(1)
    sum_cores(1)
    activate(0)
    activate(1)
    spread_core(0)
    spread_core(1)
    results(0)
    results(1)
    sum_x(1)
    sum_x(0)
    go_home(1)
    go_home(0)
    local(g_src.at[0], home_hbm.at[0], out_sem.at[4])
    for copy in kept:
        copy.wait()
    for copy in sent:
        copy.wait_send()
    for k in range(1, 8):
        gc(k, 1).wait_recv()


def finish(
    home_hbm, slots_hbm, hid_hbm, dy_hbm, out_hbm, grad_hbm, down_hbm,
    home_ref, slots_ref, hid_ref, dy_ref, out_ref, grad_ref, down_buf, in_sem, sem,
):
    rows, units = hid_ref.shape
    feat = out_ref.shape[1]
    step = units // 4
    inputs = [
        pltpu.make_async_copy(src, dst, in_sem.at[i])
        for i, (src, dst) in enumerate(
            ((hid_hbm, hid_ref), (dy_hbm, dy_ref), (home_hbm, home_ref), (slots_hbm, slots_ref))
        )
    ]
    for copy in inputs:
        copy.start()
    copies = []

    def put(src, dst):
        copies.append(pltpu.make_async_copy(src, dst, sem.at[len(copies)]))
        copies[-1].start()

    inputs[0].wait()
    inputs[1].wait()
    for i in range(4):
        own = pl.ds(i * step, step)
        down_buf[own, :] = dot(hid_ref[:, own], dy_ref[...], ((0,), (0,))).astype(BF16)
        put(down_buf.at[own, :], down_hbm.at[own, :])
    inputs[2].wait()
    inputs[3].wait()
    home = home_ref[...].reshape(EXPERTS * SLOT, 2 * feat).astype(F32)
    high = lax.Precision.HIGHEST
    out_ref[...] = dot(slots_ref[0], home[:, :feat], ((0,), (0,)), high).astype(BF16)
    put(out_ref, out_hbm)
    grad_ref[...] = dot(slots_ref[1], home[:, feat:], ((0,), (0,)), high).astype(BF16)
    put(grad_ref, grad_hbm)
    for copy in copies:
        copy.wait()


def per_device(tokens, cotangent, expert_ids, gate_weights, w_gate, w_up, w_down):
    tok_rows, feat = tokens.shape
    wide, units = w_gate.shape
    planes = lax.axis_size("expert") // EXPERTS
    cap_rows = EXPERTS * CAP
    rows = planes * cap_rows
    half = rows // 2
    hbm = pl.BlockSpec(memory_space=pl.ANY)
    dma = pltpu.SemaphoreType.DMA
    block = (EXPERTS, SLOT, 2 * feat)
    part = cap_rows // 2
    home, slots, hidden, dy_rows = pl.pallas_call(
        kernel,
        out_shape=(
            jax.ShapeDtypeStruct(block, BF16),
            jax.ShapeDtypeStruct((2, EXPERTS * SLOT, tok_rows), F32),
            jax.ShapeDtypeStruct((rows, units), BF16),
            jax.ShapeDtypeStruct((rows, wide), BF16),
        ),
        in_specs=[hbm] * 7,
        out_specs=(hbm, hbm, hbm, hbm),
        scratch_shapes=[
            pltpu.VMEM((2, tok_rows), jnp.int32), pltpu.VMEM((2, tok_rows), F32),
            pltpu.VMEM((tok_rows, feat), BF16), pltpu.VMEM((tok_rows, feat), BF16), dma((4,)),
            pltpu.VMEM((wide, units), BF16), pltpu.VMEM((wide, units), BF16),
            pltpu.VMEM((units, wide), BF16), dma((3,)),
            pltpu.VMEM(block, BF16), pltpu.VMEM((len(RELAYS),) + block[1:], BF16),
            pltpu.VMEM(block, BF16), dma((len(ARRIVALS),)), dma((len(ARRIVALS),)),
            pltpu.VMEM((4, 2, planes, part, 2 * feat), BF16),
            dma((2, 3)), dma((2, 3)), dma((2, 4, 3)), dma((2, 4, 3)),
            pltpu.VMEM((2, 4, half, 384), F32), pltpu.VMEM((2, 4, half // 2, 384), F32), dma((2, 4)), dma((2, 4)),
            pltpu.VMEM((2, half // 2, 384), F32),
            pltpu.VMEM((2, 3, half // 2, 384), BF16), pltpu.VMEM((2, 3, half // 2, 384), BF16),
            dma((2, 3)), dma((2, 3)),
            pltpu.VMEM((2, 4, 2, half // 2, 384), BF16), dma((2, 3)), dma((2, 3)), dma((2, 4)), dma((2, 4)),
            pltpu.VMEM((2, 4, half, 2 * feat), F32), pltpu.VMEM((2, 3, half, 2 * feat), BF16),
            pltpu.VMEM((2, 3, half, 2 * feat), BF16), dma((2, 3)), dma((2, 3)),
            pltpu.VMEM((2, planes, part, 2 * feat), F32),
            pltpu.VMEM((2, 3, part, 2 * feat), BF16), pltpu.VMEM((2, 3, part, 2 * feat), BF16),
            dma((2, 3)), dma((2, 3)),
            pltpu.VMEM(block, BF16), dma((7,)), dma((7,)),
            pltpu.VMEM((2, EXPERTS * SLOT, tok_rows), F32),
            pltpu.VMEM((rows, units), BF16), pltpu.VMEM((rows, wide), BF16), dma((6,)),
        ],
        compiler_params=pltpu.CompilerParams(collective_id=0, has_side_effects=True),
    )(expert_ids.T, gate_weights.T, tokens, cotangent, w_gate, w_up, w_down)
    return pl.pallas_call(
        finish,
        out_shape=(
            jax.ShapeDtypeStruct((tok_rows, feat), BF16),
            jax.ShapeDtypeStruct((tok_rows, feat), BF16),
            jax.ShapeDtypeStruct((units, wide), BF16),
        ),
        in_specs=[hbm] * 4,
        out_specs=(hbm, hbm, hbm),
        scratch_shapes=[
            pltpu.VMEM(block, BF16), pltpu.VMEM((2, EXPERTS * SLOT, tok_rows), F32),
            pltpu.VMEM((rows, units), BF16), pltpu.VMEM((rows, wide), BF16),
            pltpu.VMEM((tok_rows, feat), BF16), pltpu.VMEM((tok_rows, feat), BF16),
            pltpu.VMEM((units, wide), BF16), dma((4,)), dma((6,)),
        ],
    )(home, slots, hidden, dy_rows)


def solution(mesh):
    return jax.shard_map(
        per_device,
        mesh=mesh,
        in_specs=(
            P("expert", ("dp", "tpin", "tpout")),
            P("expert", ("dp", "tpin", "tpout")),
            P("expert", None),
            P("expert", None),
            P(("dp", "tpin"), ("expert", "tpout")),
            P(("dp", "tpin"), ("expert", "tpout")),
            P(("expert", "tpout"), ("dp", "tpin")),
        ),
        out_specs=(
            P("expert", ("dp", "tpin", "tpout")),
            P("expert", ("dp", "tpin", "tpout")),
            P(("expert", "tpout"), ("dp", "tpin")),
        ),
        check_vma=False,
    )
```

```python
import jax
import jax.numpy as jnp
from jax import lax
from jax.experimental import pallas as pl
from jax.experimental.pallas import tpu as pltpu
from jax.sharding import PartitionSpec as P

EXPERTS = 8
HID = 8192
CAP = 6
SLOT = 8
MESH = pl.DeviceIdType.MESH
F32 = jnp.float32
BF16 = jnp.bfloat16

HOPS = (0, 1, 2, 3, 0, 3, 2, 1)
AHEAD = (0, 1, 1, 1, 0, -1, -1, -1)
ARRIVALS = tuple((k, h) for k in range(1, 8) for h in range(1, HOPS[k] + 1))
RELAYS = tuple((k, h) for h in (1, 2) for k in (3, 5, 2, 6) if HOPS[k] > h)
PLACE = (0, 1, 3, 5, 7, 6, 4, 2)


def dot(a, b, contract=((1,), (0,)), precision=None):
    return lax.dot_general(
        a, b, (contract, ((), ())), preferred_element_type=F32, precision=precision
    )


def kernel(
    ids_hbm, gw_hbm, tok_hbm, cot_hbm, wg_hbm, wu_hbm, wd_hbm,
    home_hbm, slots_hbm, down_hbm,
    ids_ref, gw_ref, tok_ref, cot_ref, in_sem,
    wg, wu, wd, w_sem,
    a_src, a_relay, a_dst, a_send, a_recv, far_relay, far_send, far_recv,
    xg, b_zsend, b_zrecv, b_xsend, b_xrecv,
    p_mine, d1_dst, d1_send, d1_recv,
    d2_own, d2_src, d2_dst, d2_send, d2_recv,
    h_all, d3_send, d3_recv, d4_send, d4_recv,
    f_mine, f_src, f_dst, f_send, f_recv,
    z_sum, z_src, z_dst, z_send, z_recv,
    g_src, g_send, g_recv,
    slot_buf, hid_buf, dy_buf, down_buf, out_sem,
):
    sent, kept = [], []

    z = lax.axis_index("expert")
    x = lax.axis_index("tpout")
    y_hi = lax.axis_index("tpin")
    dp = lax.axis_index("dp")
    planes = lax.axis_size("expert") // EXPERTS
    group, plane = z // planes, z % planes
    core = dp % 2
    y = y_hi * 2 + dp // 2
    side = 1 - 2 * core
    xs = lax.axis_size("tpout")

    def at_group(step):
        return {"expert": ((group + step + EXPERTS) % EXPERTS) * planes + plane}

    def at_plane(p):
        return {"expert": group * planes + p}

    def at_x(step):
        return {"tpout": (x + step + xs) % xs}

    def at_y(step):
        there = (y + step + 4) % 4
        return {"tpin": there // 2, "dp": (there % 2) * 2 + core}

    partner = {"dp": dp + side}
    near_planes = (plane + 1 - 2 * (plane % 2), (plane + 2) % 4, 3 - plane)

    def remote(src, dst, send, recv, device):
        return pltpu.make_async_remote_copy(
            src_ref=src, dst_ref=dst, send_sem=send, recv_sem=recv,
            device_id=device, device_id_type=MESH,
        )

    def start(copy):
        copy.start()
        sent.append(copy)

    def local(src, dst, sem):
        kept.append(pltpu.make_async_copy(src, dst, sem))
        kept[-1].start()

    barrier = pltpu.get_barrier_semaphore()
    far_way = 1 - 2 * ((group + 2) % EXPERTS // 4)
    relays_far = 1 - group // 4
    peers = [at_group(step) for step in (2 * far_way, 1, -1)] + [partner]
    peers += [at_plane(p) for p in near_planes]
    peers += [at(step) for at in (at_x, at_y) for step in (2, 1, 3)]
    for peer in peers:
        pl.semaphore_signal(barrier, inc=1, device_id=peer, device_id_type=MESH)

    @pl.when(relays_far == 1)
    def _():
        pl.semaphore_signal(barrier, inc=1, device_id=at_group(-2 * far_way), device_id_type=MESH)

    inputs = [
        pltpu.make_async_copy(src, dst, in_sem.at[i])
        for i, (src, dst) in enumerate(
            ((ids_hbm, ids_ref), (gw_hbm, gw_ref), (tok_hbm, tok_ref), (cot_hbm, cot_ref))
        )
    ]
    for copy in inputs:
        copy.start()
    weights = [
        pltpu.make_async_copy(src, dst, w_sem.at[i])
        for i, (src, dst) in enumerate(((wg_hbm, wg), (wu_hbm, wu), (wd_hbm, wd)))
    ]
    for copy in weights:
        copy.start()
    for copy in inputs:
        copy.wait()

    ahead = (ids_ref[...] + EXPERTS - group) % EXPERTS
    gw = gw_ref[...]
    tokens_n = ahead.shape[1]
    expert_row = lax.broadcasted_iota(jnp.int32, (EXPERTS, tokens_n), 0)
    hit0 = jnp.where(expert_row == ahead[0:1, :], 1.0, 0.0).astype(F32)
    hit1 = jnp.where(expert_row == ahead[1:2, :], 1.0, 0.0).astype(F32)
    hit = hit0 + hit1
    weight = hit0 * gw[0:1, :] + hit1 * gw[1:2, :]
    before = jnp.where(
        lax.broadcasted_iota(jnp.int32, (tokens_n, tokens_n), 0)
        < lax.broadcasted_iota(jnp.int32, (tokens_n, tokens_n), 1), 1.0, 0.0
    ).astype(F32)
    rank = dot(hit, before)

    def spread(v):
        return jnp.concatenate(
            [jnp.broadcast_to(v[e : e + 1, :], (SLOT, tokens_n)) for e in range(EXPERTS)], axis=0
        )

    slots_n = EXPERTS * SLOT
    slot_j = (lax.broadcasted_iota(jnp.int32, (slots_n, tokens_n), 0) % SLOT).astype(F32)
    chosen = jnp.where(spread(rank) == slot_j, spread(hit), 0.0)
    slot_weights = chosen * spread(weight)
    chosen_b = chosen.astype(BF16)
    slot_gate = jnp.sum(slot_weights, axis=1, keepdims=True)
    x_rows = dot(chosen_b, tok_ref[...])
    dy_rows = dot(chosen_b, cot_ref[...]) * slot_gate
    feat = x_rows.shape[1]
    both = jnp.concatenate([x_rows, dy_rows], axis=1)
    a_src[...] = both.reshape(EXPERTS, SLOT, 2 * feat).astype(BF16)
    a_dst[0] = a_src[0]

    slot_buf[0] = slot_weights
    slot_buf[1] = chosen
    local(slot_buf, slots_hbm, out_sem.at[1])

    pl.semaphore_wait(barrier, len(peers) + relays_far)

    def a_copy(k, h):
        src = a_src.at[k] if h == 1 else a_relay.at[RELAYS.index((k, h - 1))]
        dst = a_dst.at[PLACE[k]] if h == HOPS[k] else a_relay.at[RELAYS.index((k, h))]
        n = ARRIVALS.index((k, h))
        return remote(src, dst, a_send.at[n], a_recv.at[n], at_group(AHEAD[k]))

    def a_far(way):
        n = (1 - way) // 2
        return remote(a_src.at[4], far_relay.at[n], far_send.at[2], far_recv.at[n], at_group(2 * way))

    def a_far_end(way):
        n = (1 - way) // 2
        return remote(
            far_relay.at[n], a_dst.at[PLACE[4]], far_send.at[n], far_recv.at[2], at_group(2 * way)
        )

    def a_pass(hop):
        for k, h in RELAYS:
            if h == hop:
                a_copy(k, h).wait_recv()
                start(a_copy(k, h + 1))

    def a_end(k):
        (a_copy(k, HOPS[k]) if HOPS[k] else a_far_end(1)).wait_recv()

    cap_rows = EXPERTS * CAP
    part_rows = cap_rows // 2

    def squeeze(shape, long_axis):
        rows = lax.broadcasted_iota(jnp.int32, shape, long_axis)
        short = lax.broadcasted_iota(jnp.int32, shape, 1 - long_axis)
        return jnp.where(short // CAP * SLOT + short % CAP == rows, 1.0, 0.0).astype(BF16)

    order = (plane,) + near_planes

    def bz(c, j, whose):
        there = xg.at[x, c, whose]
        return remote(there, there, b_zsend.at[c, j - 1], b_zrecv.at[c, j - 1], at_plane(order[j]))

    def bx(c, j, step, whose):
        there = xg.at[whose, c, order[j]]
        return remote(there, there, b_xsend.at[c, j, step - 1], b_xrecv.at[c, j, step - 1], at_x(step))

    def spread_x(c, j):
        for step in (2, 1, 3):
            start(bx(c, j, step, x))

    def gather(c):
        half_in = a_dst[4 * c : 4 * c + 4].reshape(slots_n // 2, 2 * feat)
        xg[x, c, plane] = dot(squeeze((part_rows, slots_n // 2), 1), half_in).astype(BF16)
        for j in (3, 2, 1):
            start(bz(c, j, plane))
        spread_x(c, 0)

    def gather_x(c):
        for j in (1, 2, 3):
            bz(c, j, order[j]).wait_recv()
            spread_x(c, j)

    half = planes * part_rows
    core_rows = half // 2
    my_rows = pl.ds(pl.multiple_of(core * core_rows, core_rows), core_rows)
    its_rows = pl.ds(pl.multiple_of((1 - core) * core_rows, core_rows), core_rows)
    wrap_y = [(y + step) % 4 for step in range(4)]

    def d1(c, i):
        return remote(
            p_mine.at[c, wrap_y[i], its_rows], d1_dst.at[c, i], d1_send.at[c, i], d1_recv.at[c, i], partner
        )

    def products(c):
        for j in range(4):
            for step in (1, 2, 3):
                bx(c, j, step, (x - step + xs) % xs).wait_recv()
        blocks = [xg[i, c].reshape(half, 2 * feat) for i in range(4)]
        x_all = jnp.concatenate([b[:, :feat] for b in blocks], axis=1)
        dy_all = jnp.concatenate([b[:, feat:] for b in blocks], axis=1)
        parts = (
            dot(x_all, wg[...]),
            dot(x_all, wu[...]),
            dot(dy_all, wd[...], ((1,), (1,))),
        )
        for i in range(4):
            for n, part in enumerate(parts):
                p_mine[c, i, :, n * 128 : (n + 1) * 128] = part[:, i * 128 : (i + 1) * 128]
        for step in (2, 1, 3, 0):
            start(d1(c, step))
        rows = pl.ds(c * half, half)
        dy_buf[rows, :] = dy_all

    def d2(c, step):
        n = step - 1
        return remote(d2_src.at[c, n], d2_dst.at[c, n], d2_send.at[c, n], d2_recv.at[c, n], at_y(step))

    def pair_sum(c, step):
        d1(c, step).wait_recv()
        return p_mine[c, wrap_y[step], my_rows, :] + d1_dst[c, step]

    def sum_cores(c):
        for step in (2, 1, 3):
            d2_src[c, step - 1] = pair_sum(c, step).astype(BF16)
            start(d2(c, step))
        d2_own[c] = pair_sum(c, 0)

    def d3(c, step, whose):
        there = h_all.at[c, whose, core]
        return remote(there, there, d3_send.at[c, step - 1], d3_recv.at[c, step - 1], at_y(step))

    def d4(c, step, whose):
        there = h_all.at[c, wrap_y[step], whose]
        return remote(there, there, d4_send.at[c, step], d4_recv.at[c, step], partner)

    def activate(c):
        total = d2_own[c]
        for step in (1, 3, 2):
            d2(c, step).wait_recv()
            total = total + d2_dst[c, step - 1].astype(F32)
        gate, up, hidden_grad = total[:, :128], total[:, 128:256], total[:, 256:]
        sig = 1.0 / (1.0 + jnp.exp(-gate))
        hidden = (gate * sig * up).astype(BF16)
        gate_grad = (hidden_grad * up * sig * (1.0 + gate * (1.0 - sig))).astype(BF16)
        up_grad = (hidden_grad * gate * sig).astype(BF16)
        h_all[c, y, core] = jnp.concatenate([hidden, gate_grad, up_grad], axis=1)
        for step in (2, 1, 3):
            start(d3(c, step, y))
        start(d4(c, 0, core))

    def spread_core(c):
        for step in (1, 3, 2):
            d3(c, step, wrap_y[4 - step]).wait_recv()
            start(d4(c, 4 - step, core))

    def f(c, step):
        n = step - 1
        return remote(f_src.at[c, n], f_dst.at[c, n], f_send.at[c, n], f_recv.at[c, n], at_x(step))

    def results(c):
        for step in range(4):
            d4(c, step, 1 - core).wait_recv()
        acts = [h_all[c, i].reshape(half, 384) for i in range(4)]
        hidden_all = jnp.concatenate([a[:, :128] for a in acts], axis=1)
        gate_grad_all = jnp.concatenate([a[:, 128:256] for a in acts], axis=1)
        up_grad_all = jnp.concatenate([a[:, 256:] for a in acts], axis=1)
        out_rows = dot(hidden_all, wd[...])
        grad_rows = dot(gate_grad_all, wg[...], ((1,), (1,))) + dot(
            up_grad_all, wu[...], ((1,), (1,))
        )
        for i in range(4):
            cols = slice(i * feat, (i + 1) * feat)
            f_mine[c, i] = jnp.concatenate([out_rows[:, cols], grad_rows[:, cols]], axis=1)
        for step in (2, 1, 3):
            f_src[c, step - 1] = f_mine[c, (x + step) % xs].astype(BF16)
            start(f(c, step))
        rows = pl.ds(c * half, half)
        hid_buf[rows, :] = hidden_all

    def zc(c, j):
        n = j - 1
        return remote(z_src.at[c, n], z_dst.at[c, n], z_send.at[c, n], z_recv.at[c, n], at_plane(order[j]))

    def sum_x(c):
        chunk_sum = f_mine[c, x]
        for step in (1, 3, 2):
            f(c, step).wait_recv()
            chunk_sum = chunk_sum + f_dst[c, step - 1].astype(F32)
        z_sum[c] = chunk_sum.reshape(planes, part_rows, 2 * feat)
        for j in (3, 2, 1):
            z_src[c, j - 1] = z_sum[c, order[j]].astype(BF16)
            start(zc(c, j))

    def gc(k, way):
        return remote(
            g_src.at[PLACE[k]], home_hbm.at[k], g_send.at[k - 1], g_recv.at[k - 1], at_group(way * k)
        )

    def go_home(c):
        routes = z_sum[c, plane]
        for j in (1, 2, 3):
            zc(c, j).wait_recv()
            routes = routes + z_dst[c, j - 1].astype(F32)
        wide = dot(squeeze((slots_n // 2, part_rows), 0), routes.astype(BF16))
        g_src[4 * c : 4 * c + 4] = wide.reshape(EXPERTS // 2, SLOT, 2 * feat).astype(BF16)
        for k in (4, 3, 5, 6) if c else (2, 1, 7):
            start(gc(k, -1))

    start(a_far(far_way))
    for k in (3, 5, 2, 6, 1, 7):
        start(a_copy(k, 1))
    a_pass(1)

    @pl.when(relays_far == 1)
    def _():
        for way in (1, -1):
            a_far(way).wait_recv()
            a_far_end(way).start()

    a_pass(2)
    for k in (1, 7, 2):
        a_end(k)
    gather(0)
    gather_x(0)
    for k in (6, 3, 5, 4):
        a_end(k)
    gather(1)
    for copy in weights:
        copy.wait()
    products(0)
    sum_cores(0)
    gather_x(1)
    activate(0)
    products(1)
    sum_cores(1)
    spread_core(0)
    results(0)
    activate(1)
    sum_x(0)
    spread_core(1)
    results(1)
    go_home(0)
    local(g_src.at[0], home_hbm.at[0], out_sem.at[0])
    sum_x(1)
    go_home(1)
    down_buf[...] = dot(hid_buf[...], dy_buf[...], ((0,), (0,))).astype(BF16)
    local(down_buf, down_hbm, out_sem.at[2])
    for copy in sent:
        copy.wait_send()

    @pl.when(relays_far == 1)
    def _():
        for way in (1, -1):
            a_far_end(way).wait_send()

    for copy in kept:
        copy.wait()
    for k in range(1, 8):
        gc(k, 1).wait_recv()


def finish(
    home_hbm, slots_hbm, made_hbm, out_hbm, grad_hbm, down_hbm,
    home_ref, slots_ref, out_ref, grad_ref, down_buf, in_sem, made_sem, sem,
):
    feat = out_ref.shape[1]
    step = down_buf.shape[0] // 4
    inputs = [
        pltpu.make_async_copy(home_hbm, home_ref, in_sem.at[0]),
        pltpu.make_async_copy(slots_hbm, slots_ref, in_sem.at[1]),
    ]
    made, done = [], []
    for i in range(4):
        own = pl.ds(i * step, step)
        made.append(pltpu.make_async_copy(made_hbm.at[own, :], down_buf.at[own, :], made_sem.at[i]))
        done.append(pltpu.make_async_copy(down_buf.at[own, :], down_hbm.at[own, :], sem.at[i]))
    for copy in inputs + made:
        copy.start()
    for copy in inputs:
        copy.wait()
    home = home_ref[...].reshape(EXPERTS * SLOT, 2 * feat).astype(F32)
    high = lax.Precision.HIGHEST
    for came, goes in zip(made, done):
        came.wait()
        goes.start()
    out_ref[...] = dot(slots_ref[0], home[:, :feat], ((0,), (0,)), high).astype(BF16)
    done.append(pltpu.make_async_copy(out_ref, out_hbm, sem.at[4]))
    done[-1].start()
    grad_ref[...] = dot(slots_ref[1], home[:, feat:], ((0,), (0,)), high).astype(BF16)
    done.append(pltpu.make_async_copy(grad_ref, grad_hbm, sem.at[5]))
    done[-1].start()
    for copy in done:
        copy.wait()


def per_device(tokens, cotangent, expert_ids, gate_weights, w_gate, w_up, w_down):
    tok_rows, feat = tokens.shape
    wide, units = w_gate.shape
    planes = lax.axis_size("expert") // EXPERTS
    cap_rows = EXPERTS * CAP
    rows = planes * cap_rows
    half = rows // 2
    hbm = pl.BlockSpec(memory_space=pl.ANY)
    dma = pltpu.SemaphoreType.DMA
    block = (EXPERTS, SLOT, 2 * feat)
    part = cap_rows // 2
    home, slots, made = pl.pallas_call(
        kernel,
        out_shape=(
            jax.ShapeDtypeStruct(block, BF16),
            jax.ShapeDtypeStruct((2, EXPERTS * SLOT, tok_rows), F32),
            jax.ShapeDtypeStruct((units, wide), BF16),
        ),
        in_specs=[hbm] * 7,
        out_specs=(hbm, hbm, hbm),
        scratch_shapes=[
            pltpu.VMEM((2, tok_rows), jnp.int32), pltpu.VMEM((2, tok_rows), F32),
            pltpu.VMEM((tok_rows, feat), BF16), pltpu.VMEM((tok_rows, feat), BF16), dma((4,)),
            pltpu.VMEM((wide, units), BF16), pltpu.VMEM((wide, units), BF16),
            pltpu.VMEM((units, wide), BF16), dma((3,)),
            pltpu.VMEM(block, BF16), pltpu.VMEM((len(RELAYS),) + block[1:], BF16),
            pltpu.VMEM(block, BF16), dma((len(ARRIVALS),)), dma((len(ARRIVALS),)),
            pltpu.VMEM((2,) + block[1:], BF16), dma((3,)), dma((3,)),
            pltpu.VMEM((4, 2, planes, part, 2 * feat), BF16),
            dma((2, 3)), dma((2, 3)), dma((2, 4, 3)), dma((2, 4, 3)),
            pltpu.VMEM((2, 4, half, 384), F32), pltpu.VMEM((2, 4, half // 2, 384), F32), dma((2, 4)), dma((2, 4)),
            pltpu.VMEM((2, half // 2, 384), F32),
            pltpu.VMEM((2, 3, half // 2, 384), BF16), pltpu.VMEM((2, 3, half // 2, 384), BF16),
            dma((2, 3)), dma((2, 3)),
            pltpu.VMEM((2, 4, 2, half // 2, 384), BF16), dma((2, 3)), dma((2, 3)), dma((2, 4)), dma((2, 4)),
            pltpu.VMEM((2, 4, half, 2 * feat), F32), pltpu.VMEM((2, 3, half, 2 * feat), BF16),
            pltpu.VMEM((2, 3, half, 2 * feat), BF16), dma((2, 3)), dma((2, 3)),
            pltpu.VMEM((2, planes, part, 2 * feat), F32),
            pltpu.VMEM((2, 3, part, 2 * feat), BF16), pltpu.VMEM((2, 3, part, 2 * feat), BF16),
            dma((2, 3)), dma((2, 3)),
            pltpu.VMEM(block, BF16), dma((7,)), dma((7,)),
            pltpu.VMEM((2, EXPERTS * SLOT, tok_rows), F32),
            pltpu.VMEM((rows, units), BF16), pltpu.VMEM((rows, wide), BF16),
            pltpu.VMEM((units, wide), BF16), dma((3,)),
        ],
        compiler_params=pltpu.CompilerParams(collective_id=0, has_side_effects=True),
    )(expert_ids.T, gate_weights.T, tokens, cotangent, w_gate, w_up, w_down)
    return pl.pallas_call(
        finish,
        out_shape=(
            jax.ShapeDtypeStruct((tok_rows, feat), BF16),
            jax.ShapeDtypeStruct((tok_rows, feat), BF16),
            jax.ShapeDtypeStruct((units, wide), BF16),
        ),
        in_specs=[hbm] * 3,
        out_specs=(hbm, hbm, hbm),
        scratch_shapes=[
            pltpu.VMEM(block, BF16), pltpu.VMEM((2, EXPERTS * SLOT, tok_rows), F32),
            pltpu.VMEM((tok_rows, feat), BF16), pltpu.VMEM((tok_rows, feat), BF16),
            pltpu.VMEM((units, wide), BF16), dma((2,)), dma((4,)), dma((6,)),
        ],
    )(home, slots, made)


def solution(mesh):
    return jax.shard_map(
        per_device,
        mesh=mesh,
        in_specs=(
            P("expert", ("dp", "tpin", "tpout")),
            P("expert", ("dp", "tpin", "tpout")),
            P("expert", None),
            P("expert", None),
            P(("dp", "tpin"), ("expert", "tpout")),
            P(("dp", "tpin"), ("expert", "tpout")),
            P(("expert", "tpout"), ("dp", "tpin")),
        ),
        out_specs=(
            P("expert", ("dp", "tpin", "tpout")),
            P("expert", ("dp", "tpin", "tpout")),
            P(("expert", "tpout"), ("dp", "tpin")),
        ),
        check_vma=False,
    )
```

```python
import jax
import jax.numpy as jnp
from jax import lax
from jax.experimental import pallas as pl
from jax.experimental.pallas import tpu as pltpu
from jax.sharding import PartitionSpec as P

EXPERTS = 8
HID = 8192
CAP = 6
SLOT = 8
MESH = pl.DeviceIdType.MESH
F32 = jnp.float32
BF16 = jnp.bfloat16

LEGS = ((), (1,), (2,), (2, 1), (0, 0), (-2, -1), (-2,), (-1,))
FIRST = (4, 3, 5, 2, 6, 1, 7)
RELAYS = (4, 3, 5)
ARRIVALS = tuple((k, h) for k in range(1, 8) for h in range(len(LEGS[k])))
PLACE = (0, 1, 3, 5, 7, 6, 4, 2)


def dot(a, b, contract=((1,), (0,)), precision=None):
    return lax.dot_general(
        a, b, (contract, ((), ())), preferred_element_type=F32, precision=precision
    )


def kernel(
    ids_hbm, gw_hbm, tok_hbm, cot_hbm, wg_hbm, wu_hbm, wd_hbm,
    home_hbm, slots_hbm, down_hbm,
    ids_ref, gw_ref, tok_ref, cot_ref, in_sem,
    wg, wu, wd, w_sem,
    a_src, a_relay, a_dst, a_send, a_recv,
    xg, b_zsend, b_zrecv, b_xsend, b_xrecv,
    p_mine, d1_dst, d1_send, d1_recv,
    d2_own, d2_src, d2_dst, d2_send, d2_recv,
    h_all, d3_send, d3_recv, d4_send, d4_recv,
    f_src, f_dst, f_send, f_recv,
    z_sum, z_src, z_dst, z_send, z_recv,
    g_src, g_send, g_recv,
    slot_buf, hid_buf, dy_buf, down_buf, out_sem,
):
    sent, kept = [], []

    z = lax.axis_index("expert")
    x = lax.axis_index("tpout")
    y_hi = lax.axis_index("tpin")
    dp = lax.axis_index("dp")
    planes = lax.axis_size("expert") // EXPERTS
    group, plane = z // planes, z % planes
    core = dp % 2
    y = y_hi * 2 + dp // 2
    side = 1 - 2 * core
    xs = lax.axis_size("tpout")

    def at_group(step):
        return {"expert": ((group + step + EXPERTS) % EXPERTS) * planes + plane}

    def at_plane(p):
        return {"expert": group * planes + p}

    def at_x(step):
        return {"tpout": (x + step + xs) % xs}

    def at_y(step):
        there = (y + step + 4) % 4
        return {"tpin": there // 2, "dp": (there % 2) * 2 + core}

    partner = {"dp": dp + side}
    near_planes = (plane + 1 - 2 * (plane % 2), (plane + 2) % 4, 3 - plane)

    def remote(src, dst, send, recv, device):
        return pltpu.make_async_remote_copy(
            src_ref=src, dst_ref=dst, send_sem=send, recv_sem=recv,
            device_id=device, device_id_type=MESH,
        )

    def start(copy):
        copy.start()
        sent.append(copy)

    def local(src, dst, sem):
        kept.append(pltpu.make_async_copy(src, dst, sem))
        kept[-1].start()

    barrier = pltpu.get_barrier_semaphore()
    peers = [at_group(step) for step in (2, -2, 1, -1)] + [partner]
    peers += [at_plane(p) for p in near_planes]
    peers += [at(step) for at in (at_x, at_y) for step in (2, 1, 3)]
    for peer in peers:
        pl.semaphore_signal(barrier, inc=1, device_id=peer, device_id_type=MESH)
    inputs = [
        pltpu.make_async_copy(src, dst, in_sem.at[i])
        for i, (src, dst) in enumerate(
            ((ids_hbm, ids_ref), (gw_hbm, gw_ref), (tok_hbm, tok_ref), (cot_hbm, cot_ref))
        )
    ]
    for copy in inputs:
        copy.start()
    weights = [
        pltpu.make_async_copy(src, dst, w_sem.at[i])
        for i, (src, dst) in enumerate(((wg_hbm, wg), (wu_hbm, wu), (wd_hbm, wd)))
    ]
    for copy in weights:
        copy.start()
    for copy in inputs:
        copy.wait()

    ahead = (ids_ref[...] + EXPERTS - group) % EXPERTS
    gw = gw_ref[...]
    tokens_n = ahead.shape[1]
    expert_row = lax.broadcasted_iota(jnp.int32, (EXPERTS, tokens_n), 0)
    hit0 = jnp.where(expert_row == ahead[0:1, :], 1.0, 0.0).astype(F32)
    hit1 = jnp.where(expert_row == ahead[1:2, :], 1.0, 0.0).astype(F32)
    hit = hit0 + hit1
    weight = hit0 * gw[0:1, :] + hit1 * gw[1:2, :]
    before = jnp.where(
        lax.broadcasted_iota(jnp.int32, (tokens_n, tokens_n), 0)
        < lax.broadcasted_iota(jnp.int32, (tokens_n, tokens_n), 1), 1.0, 0.0
    ).astype(F32)
    rank = dot(hit, before)

    def spread(v):
        return jnp.concatenate(
            [jnp.broadcast_to(v[e : e + 1, :], (SLOT, tokens_n)) for e in range(EXPERTS)], axis=0
        )

    slots_n = EXPERTS * SLOT
    slot_j = (lax.broadcasted_iota(jnp.int32, (slots_n, tokens_n), 0) % SLOT).astype(F32)
    chosen = jnp.where(spread(rank) == slot_j, spread(hit), 0.0)
    slot_weights = chosen * spread(weight)
    chosen_b = chosen.astype(BF16)
    slot_gate = jnp.sum(slot_weights, axis=1, keepdims=True)
    x_rows = dot(chosen_b, tok_ref[...])
    dy_rows = dot(chosen_b, cot_ref[...]) * slot_gate
    feat = x_rows.shape[1]
    both = jnp.concatenate([x_rows, dy_rows], axis=1)
    a_src[...] = both.reshape(EXPERTS, SLOT, 2 * feat).astype(BF16)
    a_dst[0] = a_src[0]

    slot_buf[0] = slot_weights
    slot_buf[1] = chosen
    local(slot_buf, slots_hbm, out_sem.at[1])

    pl.semaphore_wait(barrier, len(peers))

    def a_copy(k, h):
        src = a_relay.at[RELAYS.index(k)] if h else a_src.at[k]
        dst = a_dst.at[PLACE[k]] if h == len(LEGS[k]) - 1 else a_relay.at[RELAYS.index(k)]
        n = ARRIVALS.index((k, h))
        return remote(src, dst, a_send.at[n], a_recv.at[n], at_group(LEGS[k][h] or 2 * side))

    def a_end(k):
        a_copy(k, len(LEGS[k]) - 1).wait_recv()

    cap_rows = EXPERTS * CAP
    part_rows = cap_rows // 2

    def squeeze(shape, long_axis):
        rows = lax.broadcasted_iota(jnp.int32, shape, long_axis)
        short = lax.broadcasted_iota(jnp.int32, shape, 1 - long_axis)
        return jnp.where(short // CAP * SLOT + short % CAP == rows, 1.0, 0.0).astype(BF16)

    order = (plane,) + near_planes

    def bz(c, j, whose):
        there = xg.at[x, c, whose]
        return remote(there, there, b_zsend.at[c, j - 1], b_zrecv.at[c, j - 1], at_plane(order[j]))

    def bx(c, j, step, whose):
        there = xg.at[whose, c, order[j]]
        return remote(there, there, b_xsend.at[c, j, step - 1], b_xrecv.at[c, j, step - 1], at_x(step))

    def spread_x(c, j):
        for step in (2, 1, 3):
            start(bx(c, j, step, x))

    def gather(c):
        half_in = a_dst[4 * c : 4 * c + 4].reshape(slots_n // 2, 2 * feat)
        xg[x, c, plane] = dot(squeeze((part_rows, slots_n // 2), 1), half_in).astype(BF16)
        for j in (3, 2, 1):
            start(bz(c, j, plane))
        spread_x(c, 0)

    def gather_x(c):
        for j in (1, 2, 3):
            bz(c, j, order[j]).wait_recv()
            spread_x(c, j)

    half = planes * part_rows
    core_rows = half // 2
    my_rows = pl.ds(pl.multiple_of(core * core_rows, core_rows), core_rows)
    its_rows = pl.ds(pl.multiple_of((1 - core) * core_rows, core_rows), core_rows)
    wrap_y = [(y + step) % 4 for step in range(4)]

    def d1(c, i):
        return remote(
            p_mine.at[c, wrap_y[i], its_rows], d1_dst.at[c, i], d1_send.at[c, i], d1_recv.at[c, i], partner
        )

    def products(c):
        for j in range(4):
            for step in (1, 2, 3):
                bx(c, j, step, (x - step + xs) % xs).wait_recv()
        blocks = [xg[i, c].reshape(half, 2 * feat) for i in range(4)]
        x_all = jnp.concatenate([b[:, :feat] for b in blocks], axis=1)
        dy_all = jnp.concatenate([b[:, feat:] for b in blocks], axis=1)
        parts = (
            dot(x_all, wg[...]),
            dot(x_all, wu[...]),
            dot(dy_all, wd[...], ((1,), (1,))),
        )
        for i in range(4):
            for n, part in enumerate(parts):
                p_mine[c, i, :, n * 128 : (n + 1) * 128] = part[:, i * 128 : (i + 1) * 128]
        for step in (2, 1, 3, 0):
            start(d1(c, step))
        rows = pl.ds(c * half, half)
        dy_buf[rows, :] = dy_all

    def d2(c, step):
        n = step - 1
        return remote(d2_src.at[c, n], d2_dst.at[c, n], d2_send.at[c, n], d2_recv.at[c, n], at_y(step))

    def pair_sum(c, step):
        d1(c, step).wait_recv()
        return p_mine[c, wrap_y[step], my_rows, :] + d1_dst[c, step]

    def sum_cores(c):
        for step in (2, 1, 3):
            d2_src[c, step - 1] = pair_sum(c, step).astype(BF16)
            start(d2(c, step))
        d2_own[c] = pair_sum(c, 0)

    def d3(c, step, whose):
        there = h_all.at[c, whose, core]
        return remote(there, there, d3_send.at[c, step - 1], d3_recv.at[c, step - 1], at_y(step))

    def d4(c, step, whose):
        there = h_all.at[c, wrap_y[step], whose]
        return remote(there, there, d4_send.at[c, step], d4_recv.at[c, step], partner)

    def activate(c):
        total = d2_own[c]
        for step in (1, 3, 2):
            d2(c, step).wait_recv()
            total = total + d2_dst[c, step - 1].astype(F32)
        gate, up, hidden_grad = total[:, :128], total[:, 128:256], total[:, 256:]
        sig = 1.0 / (1.0 + jnp.exp(-gate))
        hidden = (gate * sig * up).astype(BF16)
        gate_grad = (hidden_grad * up * sig * (1.0 + gate * (1.0 - sig))).astype(BF16)
        up_grad = (hidden_grad * gate * sig).astype(BF16)
        h_all[c, y, core] = jnp.concatenate([hidden, gate_grad, up_grad], axis=1)
        for step in (2, 1, 3):
            start(d3(c, step, y))
        start(d4(c, 0, core))

    def spread_core(c):
        for step in (1, 3, 2):
            d3(c, step, wrap_y[4 - step]).wait_recv()
            start(d4(c, 4 - step, core))

    def f(c, step):
        n = step - 1
        return remote(f_src.at[c, (x + step) % xs], f_dst.at[c, n], f_send.at[c, n], f_recv.at[c, n], at_x(step))

    def results(c):
        for step in range(4):
            d4(c, step, 1 - core).wait_recv()
        acts = [h_all[c, i].reshape(half, 384) for i in range(4)]
        hidden_all = jnp.concatenate([a[:, :128] for a in acts], axis=1)
        gate_grad_all = jnp.concatenate([a[:, 128:256] for a in acts], axis=1)
        up_grad_all = jnp.concatenate([a[:, 256:] for a in acts], axis=1)
        out_rows = dot(hidden_all, wd[...])
        grad_rows = dot(gate_grad_all, wg[...], ((1,), (1,))) + dot(
            up_grad_all, wu[...], ((1,), (1,))
        )
        for i in range(4):
            cols = slice(i * feat, (i + 1) * feat)
            f_src[c, i] = jnp.concatenate([out_rows[:, cols], grad_rows[:, cols]], axis=1).astype(BF16)
        for step in (2, 1, 3):
            start(f(c, step))
        rows = pl.ds(c * half, half)
        hid_buf[rows, :] = hidden_all

    def zc(c, j):
        n = j - 1
        return remote(z_src.at[c, n], z_dst.at[c, n], z_send.at[c, n], z_recv.at[c, n], at_plane(order[j]))

    def sum_x(c):
        chunk_sum = f_src[c, x].astype(F32)
        for step in (1, 3, 2):
            f(c, step).wait_recv()
            chunk_sum = chunk_sum + f_dst[c, step - 1].astype(F32)
        z_sum[c] = chunk_sum.reshape(planes, part_rows, 2 * feat)
        for j in (3, 2, 1):
            z_src[c, j - 1] = z_sum[c, order[j]].astype(BF16)
            start(zc(c, j))

    def gc(k, way):
        return remote(
            g_src.at[PLACE[k]], home_hbm.at[k], g_send.at[k - 1], g_recv.at[k - 1], at_group(way * k)
        )

    def go_home(c):
        routes = z_sum[c, plane]
        for j in (1, 2, 3):
            zc(c, j).wait_recv()
            routes = routes + z_dst[c, j - 1].astype(F32)
        wide = dot(squeeze((slots_n // 2, part_rows), 0), routes.astype(BF16))
        g_src[4 * c : 4 * c + 4] = wide.reshape(EXPERTS // 2, SLOT, 2 * feat).astype(BF16)
        for k in (4, 3, 5, 6) if c else (2, 1, 7):
            start(gc(k, -1))

    for k in FIRST:
        start(a_copy(k, 0))
    for k in RELAYS:
        a_copy(k, 0).wait_recv()
        start(a_copy(k, 1))
    for k in (1, 7, 2):
        a_end(k)
    gather(0)
    gather_x(0)
    for k in (6, 3, 5, 4):
        a_end(k)
    gather(1)
    for copy in weights:
        copy.wait()
    products(0)
    sum_cores(0)
    gather_x(1)
    activate(0)
    products(1)
    sum_cores(1)
    spread_core(0)
    results(0)
    activate(1)
    sum_x(0)
    spread_core(1)
    results(1)
    go_home(0)
    local(g_src.at[0], home_hbm.at[0], out_sem.at[0])
    sum_x(1)
    go_home(1)
    down_buf[...] = dot(hid_buf[...], dy_buf[...], ((0,), (0,))).astype(BF16)
    local(down_buf, down_hbm, out_sem.at[2])
    for copy in sent:
        copy.wait_send()
    for copy in kept:
        copy.wait()
    for k in range(1, 8):
        gc(k, 1).wait_recv()


def finish(
    home_hbm, slots_hbm, made_hbm, out_hbm, grad_hbm, down_hbm,
    home_ref, slots_ref, out_ref, grad_ref, down_buf, in_sem, made_sem, sem,
):
    feat = out_ref.shape[1]
    step = down_buf.shape[0] // 4
    inputs = [
        pltpu.make_async_copy(home_hbm, home_ref, in_sem.at[0]),
        pltpu.make_async_copy(slots_hbm, slots_ref, in_sem.at[1]),
    ]
    made, done = [], []
    for i in range(4):
        own = pl.ds(i * step, step)
        made.append(pltpu.make_async_copy(made_hbm.at[own, :], down_buf.at[own, :], made_sem.at[i]))
        done.append(pltpu.make_async_copy(down_buf.at[own, :], down_hbm.at[own, :], sem.at[i]))
    for copy in inputs + made:
        copy.start()
    for copy in inputs:
        copy.wait()
    home = home_ref[...].reshape(EXPERTS * SLOT, 2 * feat).astype(F32)
    high = lax.Precision.HIGHEST
    for came, goes in zip(made, done):
        came.wait()
        goes.start()
    out_ref[...] = dot(slots_ref[0], home[:, :feat], ((0,), (0,)), high).astype(BF16)
    done.append(pltpu.make_async_copy(out_ref, out_hbm, sem.at[4]))
    done[-1].start()
    grad_ref[...] = dot(slots_ref[1], home[:, feat:], ((0,), (0,)), high).astype(BF16)
    done.append(pltpu.make_async_copy(grad_ref, grad_hbm, sem.at[5]))
    done[-1].start()
    for copy in done:
        copy.wait()


def per_device(tokens, cotangent, expert_ids, gate_weights, w_gate, w_up, w_down):
    tok_rows, feat = tokens.shape
    wide, units = w_gate.shape
    planes = lax.axis_size("expert") // EXPERTS
    cap_rows = EXPERTS * CAP
    rows = planes * cap_rows
    half = rows // 2
    hbm = pl.BlockSpec(memory_space=pl.ANY)
    dma = pltpu.SemaphoreType.DMA
    block = (EXPERTS, SLOT, 2 * feat)
    part = cap_rows // 2
    home, slots, made = pl.pallas_call(
        kernel,
        out_shape=(
            jax.ShapeDtypeStruct(block, BF16),
            jax.ShapeDtypeStruct((2, EXPERTS * SLOT, tok_rows), F32),
            jax.ShapeDtypeStruct((units, wide), BF16),
        ),
        in_specs=[hbm] * 7,
        out_specs=(hbm, hbm, hbm),
        scratch_shapes=[
            pltpu.VMEM((2, tok_rows), jnp.int32), pltpu.VMEM((2, tok_rows), F32),
            pltpu.VMEM((tok_rows, feat), BF16), pltpu.VMEM((tok_rows, feat), BF16), dma((4,)),
            pltpu.VMEM((wide, units), BF16), pltpu.VMEM((wide, units), BF16),
            pltpu.VMEM((units, wide), BF16), dma((3,)),
            pltpu.VMEM(block, BF16), pltpu.VMEM((len(RELAYS),) + block[1:], BF16),
            pltpu.VMEM(block, BF16), dma((len(ARRIVALS),)), dma((len(ARRIVALS),)),
            pltpu.VMEM((4, 2, planes, part, 2 * feat), BF16),
            dma((2, 3)), dma((2, 3)), dma((2, 4, 3)), dma((2, 4, 3)),
            pltpu.VMEM((2, 4, half, 384), F32), pltpu.VMEM((2, 4, half // 2, 384), F32), dma((2, 4)), dma((2, 4)),
            pltpu.VMEM((2, half // 2, 384), F32),
            pltpu.VMEM((2, 3, half // 2, 384), BF16), pltpu.VMEM((2, 3, half // 2, 384), BF16),
            dma((2, 3)), dma((2, 3)),
            pltpu.VMEM((2, 4, 2, half // 2, 384), BF16), dma((2, 3)), dma((2, 3)), dma((2, 4)), dma((2, 4)),
            pltpu.VMEM((2, 4, half, 2 * feat), BF16),
            pltpu.VMEM((2, 3, half, 2 * feat), BF16), dma((2, 3)), dma((2, 3)),
            pltpu.VMEM((2, planes, part, 2 * feat), F32),
            pltpu.VMEM((2, 3, part, 2 * feat), BF16), pltpu.VMEM((2, 3, part, 2 * feat), BF16),
            dma((2, 3)), dma((2, 3)),
            pltpu.VMEM(block, BF16), dma((7,)), dma((7,)),
            pltpu.VMEM((2, EXPERTS * SLOT, tok_rows), F32),
            pltpu.VMEM((rows, units), BF16), pltpu.VMEM((rows, wide), BF16),
            pltpu.VMEM((units, wide), BF16), dma((3,)),
        ],
        compiler_params=pltpu.CompilerParams(collective_id=0, has_side_effects=True),
    )(expert_ids.T, gate_weights.T, tokens, cotangent, w_gate, w_up, w_down)
    return pl.pallas_call(
        finish,
        out_shape=(
            jax.ShapeDtypeStruct((tok_rows, feat), BF16),
            jax.ShapeDtypeStruct((tok_rows, feat), BF16),
            jax.ShapeDtypeStruct((units, wide), BF16),
        ),
        in_specs=[hbm] * 3,
        out_specs=(hbm, hbm, hbm),
        scratch_shapes=[
            pltpu.VMEM(block, BF16), pltpu.VMEM((2, EXPERTS * SLOT, tok_rows), F32),
            pltpu.VMEM((tok_rows, feat), BF16), pltpu.VMEM((tok_rows, feat), BF16),
            pltpu.VMEM((units, wide), BF16), dma((2,)), dma((4,)), dma((6,)),
        ],
    )(home, slots, made)


def solution(mesh):
    return jax.shard_map(
        per_device,
        mesh=mesh,
        in_specs=(
            P("expert", ("dp", "tpin", "tpout")),
            P("expert", ("dp", "tpin", "tpout")),
            P("expert", None),
            P("expert", None),
            P(("dp", "tpin"), ("expert", "tpout")),
            P(("dp", "tpin"), ("expert", "tpout")),
            P(("expert", "tpout"), ("dp", "tpin")),
        ),
        out_specs=(
            P("expert", ("dp", "tpin", "tpout")),
            P("expert", ("dp", "tpin", "tpout")),
            P(("expert", "tpout"), ("dp", "tpin")),
        ),
        check_vma=False,
    )
```

```python
import jax
import jax.numpy as jnp
from jax import lax
from jax.experimental import pallas as pl
from jax.experimental.pallas import tpu as pltpu
from jax.sharding import PartitionSpec as P

EXPERTS = 8
HID = 8192
CAP = 6
SLOT = 8
MESH = pl.DeviceIdType.MESH
F32 = jnp.float32
BF16 = jnp.bfloat16

LEGS = ((), (1,), (2,), (2, 1), (0, 0), (-2, -1), (-2,), (-1,))
FIRST = (4, 3, 5, 2, 6, 1, 7)
RELAYS = (4, 3, 5)
ARRIVALS = tuple((k, h) for k in range(1, 8) for h in range(len(LEGS[k])))
PLACE = (0, 1, 3, 5, 7, 6, 4, 2)


def dot(a, b, contract=((1,), (0,)), precision=None):
    return lax.dot_general(
        a, b, (contract, ((), ())), preferred_element_type=F32, precision=precision
    )


def kernel(
    ids_hbm, gw_hbm, tok_hbm, cot_hbm, wg_hbm, wu_hbm, wd_hbm,
    home_hbm, slots_hbm, down_hbm,
    ids_ref, gw_ref, tok_ref, cot_ref, in_sem,
    wg, wu, wd, w_sem,
    a_src, a_relay, a_dst, a_send, a_recv,
    xg, b_zsend, b_zrecv, b_xsend, b_xrecv,
    p_mine, d1_dst, d1_send, d1_recv,
    d2_own, d2_src, d2_dst, d2_send, d2_recv,
    h_all, d3_send, d3_recv, d4_send, d4_recv,
    f_src, f_dst, f_send, f_recv,
    z_sum, z_src, z_dst, z_send, z_recv,
    g_src, g_send, g_recv,
    slot_buf, hid_buf, dy_buf, down_buf, out_sem,
):
    sent, kept = [], []

    z = lax.axis_index("expert")
    x = lax.axis_index("tpout")
    y_hi = lax.axis_index("tpin")
    dp = lax.axis_index("dp")
    planes = lax.axis_size("expert") // EXPERTS
    group, plane = z // planes, z % planes
    core = dp % 2
    y = y_hi * 2 + dp // 2
    side = 1 - 2 * core
    xs = lax.axis_size("tpout")

    def at_group(step):
        return {"expert": ((group + step + EXPERTS) % EXPERTS) * planes + plane}

    def at_plane(p):
        return {"expert": group * planes + p}

    def at_x(step):
        return {"tpout": (x + step + xs) % xs}

    def at_y(step, other=0):
        there = (y + step + 4) % 4
        return {"tpin": there // 2, "dp": (there % 2) * 2 + (core + other) % 2}

    partner = {"dp": dp + side}
    near_planes = (plane + 1 - 2 * (plane % 2), (plane + 2) % 4, 3 - plane)

    def remote(src, dst, send, recv, device):
        return pltpu.make_async_remote_copy(
            src_ref=src, dst_ref=dst, send_sem=send, recv_sem=recv,
            device_id=device, device_id_type=MESH,
        )

    def start(copy):
        copy.start()
        sent.append(copy)

    def local(src, dst, sem):
        kept.append(pltpu.make_async_copy(src, dst, sem))
        kept[-1].start()

    barrier = pltpu.get_barrier_semaphore()
    peers = [at_group(step) for step in (2, -2, 1, -1)] + [partner]
    peers += [at_plane(p) for p in near_planes]
    peers += [at(step) for at in (at_x, at_y) for step in (2, 1, 3)]
    peers += [at_y(step, 1) for step in (2, 1, 3)]
    for peer in peers:
        pl.semaphore_signal(barrier, inc=1, device_id=peer, device_id_type=MESH)
    inputs = [
        pltpu.make_async_copy(src, dst, in_sem.at[i])
        for i, (src, dst) in enumerate(
            ((ids_hbm, ids_ref), (gw_hbm, gw_ref), (tok_hbm, tok_ref), (cot_hbm, cot_ref))
        )
    ]
    for copy in inputs:
        copy.start()
    weights = [
        pltpu.make_async_copy(src, dst, w_sem.at[i])
        for i, (src, dst) in enumerate(((wg_hbm, wg), (wu_hbm, wu), (wd_hbm, wd)))
    ]
    for copy in weights:
        copy.start()
    for copy in inputs:
        copy.wait()

    ahead = (ids_ref[...] + EXPERTS - group) % EXPERTS
    gw = gw_ref[...]
    tokens_n = ahead.shape[1]
    expert_row = lax.broadcasted_iota(jnp.int32, (EXPERTS, tokens_n), 0)
    hit0 = jnp.where(expert_row == ahead[0:1, :], 1.0, 0.0).astype(F32)
    hit1 = jnp.where(expert_row == ahead[1:2, :], 1.0, 0.0).astype(F32)
    hit = hit0 + hit1
    weight = hit0 * gw[0:1, :] + hit1 * gw[1:2, :]
    before = jnp.where(
        lax.broadcasted_iota(jnp.int32, (tokens_n, tokens_n), 0)
        < lax.broadcasted_iota(jnp.int32, (tokens_n, tokens_n), 1), 1.0, 0.0
    ).astype(F32)
    rank = dot(hit, before)

    def spread(v):
        return jnp.concatenate(
            [jnp.broadcast_to(v[e : e + 1, :], (SLOT, tokens_n)) for e in range(EXPERTS)], axis=0
        )

    slots_n = EXPERTS * SLOT
    slot_j = (lax.broadcasted_iota(jnp.int32, (slots_n, tokens_n), 0) % SLOT).astype(F32)
    chosen = jnp.where(spread(rank) == slot_j, spread(hit), 0.0)
    slot_weights = chosen * spread(weight)
    chosen_b = chosen.astype(BF16)
    slot_gate = jnp.sum(slot_weights, axis=1, keepdims=True)
    x_rows = dot(chosen_b, tok_ref[...])
    dy_rows = dot(chosen_b, cot_ref[...]) * slot_gate
    feat = x_rows.shape[1]
    both = jnp.concatenate([x_rows, dy_rows], axis=1)
    a_src[...] = both.reshape(EXPERTS, SLOT, 2 * feat).astype(BF16)
    a_dst[0] = a_src[0]

    slot_buf[0] = slot_weights
    slot_buf[1] = chosen
    local(slot_buf, slots_hbm, out_sem.at[1])

    pl.semaphore_wait(barrier, len(peers))

    def a_copy(k, h):
        src = a_relay.at[RELAYS.index(k)] if h else a_src.at[k]
        dst = a_dst.at[PLACE[k]] if h == len(LEGS[k]) - 1 else a_relay.at[RELAYS.index(k)]
        n = ARRIVALS.index((k, h))
        return remote(src, dst, a_send.at[n], a_recv.at[n], at_group(LEGS[k][h] or 2 * side))

    def a_end(k):
        a_copy(k, len(LEGS[k]) - 1).wait_recv()

    cap_rows = EXPERTS * CAP
    part_rows = cap_rows // 2

    def squeeze(shape, long_axis):
        rows = lax.broadcasted_iota(jnp.int32, shape, long_axis)
        short = lax.broadcasted_iota(jnp.int32, shape, 1 - long_axis)
        return jnp.where(short // CAP * SLOT + short % CAP == rows, 1.0, 0.0).astype(BF16)

    order = (plane,) + near_planes

    def bz(c, j, whose):
        there = xg.at[x, c, whose]
        return remote(there, there, b_zsend.at[c, j - 1], b_zrecv.at[c, j - 1], at_plane(order[j]))

    def bx(c, j, step, whose):
        there = xg.at[whose, c, order[j]]
        return remote(there, there, b_xsend.at[c, j, step - 1], b_xrecv.at[c, j, step - 1], at_x(step))

    def spread_x(c, j):
        for step in (2, 1, 3):
            start(bx(c, j, step, x))

    def gather(c):
        half_in = a_dst[4 * c : 4 * c + 4].reshape(slots_n // 2, 2 * feat)
        xg[x, c, plane] = dot(squeeze((part_rows, slots_n // 2), 1), half_in).astype(BF16)
        for j in (3, 2, 1):
            start(bz(c, j, plane))
        spread_x(c, 0)

    def gather_x(c):
        for j in (1, 2, 3):
            bz(c, j, order[j]).wait_recv()
            spread_x(c, j)

    half = planes * part_rows
    core_rows = half // 2
    my_rows = pl.ds(pl.multiple_of(core * core_rows, core_rows), core_rows)
    its_rows = pl.ds(pl.multiple_of((1 - core) * core_rows, core_rows), core_rows)
    wrap_y = [(y + step) % 4 for step in range(4)]

    def d1(c, i):
        return remote(
            p_mine.at[c, wrap_y[i], its_rows], d1_dst.at[c, i], d1_send.at[c, i], d1_recv.at[c, i], partner
        )

    def products(c):
        for j in range(4):
            for step in (1, 2, 3):
                bx(c, j, step, (x - step + xs) % xs).wait_recv()
        blocks = [xg[i, c].reshape(half, 2 * feat) for i in range(4)]
        x_all = jnp.concatenate([b[:, :feat] for b in blocks], axis=1)
        dy_all = jnp.concatenate([b[:, feat:] for b in blocks], axis=1)
        parts = (
            dot(x_all, wg[...]),
            dot(x_all, wu[...]),
            dot(dy_all, wd[...], ((1,), (1,))),
        )
        for i in range(4):
            for n, part in enumerate(parts):
                p_mine[c, i, :, n * 128 : (n + 1) * 128] = part[:, i * 128 : (i + 1) * 128]
        for step in (2, 1, 3, 0):
            start(d1(c, step))
        rows = pl.ds(c * half, half)
        dy_buf[rows, :] = dy_all

    def d2(c, step):
        n = step - 1
        return remote(d2_src.at[c, n], d2_dst.at[c, n], d2_send.at[c, n], d2_recv.at[c, n], at_y(step))

    def pair_sum(c, step):
        d1(c, step).wait_recv()
        return p_mine[c, wrap_y[step], my_rows, :] + d1_dst[c, step]

    def sum_cores(c):
        for step in (2, 1, 3):
            d2_src[c, step - 1] = pair_sum(c, step).astype(BF16)
            start(d2(c, step))
        d2_own[c] = pair_sum(c, 0)

    def d3(c, step, other, whose):
        there = h_all.at[c, whose, core]
        n = step - 1
        return remote(
            there, there, d3_send.at[c, other, n], d3_recv.at[c, other, n], at_y(step, other)
        )

    def d3_in(c, step, other):
        there = h_all.at[c, wrap_y[4 - step], (core + other) % 2]
        n = step - 1
        return remote(
            there, there, d3_send.at[c, other, n], d3_recv.at[c, other, n], at_y(step, other)
        )

    def d4(c, whose):
        there = h_all.at[c, y, whose]
        return remote(there, there, d4_send.at[c], d4_recv.at[c], partner)

    def activate(c):
        total = d2_own[c]
        for step in (1, 3, 2):
            d2(c, step).wait_recv()
            total = total + d2_dst[c, step - 1].astype(F32)
        gate, up, hidden_grad = total[:, :128], total[:, 128:256], total[:, 256:]
        sig = 1.0 / (1.0 + jnp.exp(-gate))
        hidden = (gate * sig * up).astype(BF16)
        gate_grad = (hidden_grad * up * sig * (1.0 + gate * (1.0 - sig))).astype(BF16)
        up_grad = (hidden_grad * gate * sig).astype(BF16)
        h_all[c, y, core] = jnp.concatenate([hidden, gate_grad, up_grad], axis=1)
        for step in (2, 1, 3):
            for other in (1, 0):
                start(d3(c, step, other, y))
        start(d4(c, core))

    def f(c, step):
        n = step - 1
        return remote(f_src.at[c, (x + step) % xs], f_dst.at[c, n], f_send.at[c, n], f_recv.at[c, n], at_x(step))

    def results(c):
        d4(c, 1 - core).wait_recv()
        for step in (1, 3, 2):
            for other in (0, 1):
                d3_in(c, step, other).wait_recv()
        acts = [h_all[c, i].reshape(half, 384) for i in range(4)]
        hidden_all = jnp.concatenate([a[:, :128] for a in acts], axis=1)
        gate_grad_all = jnp.concatenate([a[:, 128:256] for a in acts], axis=1)
        up_grad_all = jnp.concatenate([a[:, 256:] for a in acts], axis=1)
        out_rows = dot(hidden_all, wd[...])
        grad_rows = dot(gate_grad_all, wg[...], ((1,), (1,))) + dot(
            up_grad_all, wu[...], ((1,), (1,))
        )
        for i in range(4):
            cols = slice(i * feat, (i + 1) * feat)
            f_src[c, i] = jnp.concatenate([out_rows[:, cols], grad_rows[:, cols]], axis=1).astype(BF16)
        for step in (2, 1, 3):
            start(f(c, step))
        rows = pl.ds(c * half, half)
        hid_buf[rows, :] = hidden_all

    def zc(c, j):
        n = j - 1
        return remote(z_src.at[c, n], z_dst.at[c, n], z_send.at[c, n], z_recv.at[c, n], at_plane(order[j]))

    def sum_x(c):
        chunk_sum = f_src[c, x].astype(F32)
        for step in (1, 3, 2):
            f(c, step).wait_recv()
            chunk_sum = chunk_sum + f_dst[c, step - 1].astype(F32)
        z_sum[c] = chunk_sum.reshape(planes, part_rows, 2 * feat)
        for j in (3, 2, 1):
            z_src[c, j - 1] = z_sum[c, order[j]].astype(BF16)
            start(zc(c, j))

    def gc(k, way):
        return remote(
            g_src.at[PLACE[k]], home_hbm.at[k], g_send.at[k - 1], g_recv.at[k - 1], at_group(way * k)
        )

    def go_home(c):
        routes = z_sum[c, plane]
        for j in (1, 2, 3):
            zc(c, j).wait_recv()
            routes = routes + z_dst[c, j - 1].astype(F32)
        wide = dot(squeeze((slots_n // 2, part_rows), 0), routes.astype(BF16))
        g_src[4 * c : 4 * c + 4] = wide.reshape(EXPERTS // 2, SLOT, 2 * feat).astype(BF16)
        for k in (4, 3, 5, 6) if c else (2, 1, 7):
            start(gc(k, -1))

    for k in FIRST:
        start(a_copy(k, 0))
    for k in RELAYS:
        a_copy(k, 0).wait_recv()
        start(a_copy(k, 1))
    for k in (1, 7, 2):
        a_end(k)
    gather(0)
    gather_x(0)
    for k in (6, 3, 5, 4):
        a_end(k)
    gather(1)
    for copy in weights:
        copy.wait()
    products(0)
    sum_cores(0)
    gather_x(1)
    activate(0)
    products(1)
    sum_cores(1)
    results(0)
    activate(1)
    sum_x(0)
    results(1)
    go_home(0)
    local(g_src.at[0], home_hbm.at[0], out_sem.at[0])
    sum_x(1)
    go_home(1)
    down_buf[...] = dot(hid_buf[...], dy_buf[...], ((0,), (0,))).astype(BF16)
    local(down_buf, down_hbm, out_sem.at[2])
    for copy in sent:
        copy.wait_send()
    for copy in kept:
        copy.wait()
    for k in range(1, 8):
        gc(k, 1).wait_recv()


def finish(
    home_hbm, slots_hbm, made_hbm, out_hbm, grad_hbm, down_hbm,
    home_ref, slots_ref, out_ref, grad_ref, down_buf, in_sem, made_sem, sem,
):
    feat = out_ref.shape[1]
    step = down_buf.shape[0] // 4
    inputs = [
        pltpu.make_async_copy(home_hbm, home_ref, in_sem.at[0]),
        pltpu.make_async_copy(slots_hbm, slots_ref, in_sem.at[1]),
    ]
    made, done = [], []
    for i in range(4):
        own = pl.ds(i * step, step)
        made.append(pltpu.make_async_copy(made_hbm.at[own, :], down_buf.at[own, :], made_sem.at[i]))
        done.append(pltpu.make_async_copy(down_buf.at[own, :], down_hbm.at[own, :], sem.at[i]))
    for copy in inputs + made:
        copy.start()
    for copy in inputs:
        copy.wait()
    home = home_ref[...].reshape(EXPERTS * SLOT, 2 * feat).astype(F32)
    high = lax.Precision.HIGHEST
    for came, goes in zip(made, done):
        came.wait()
        goes.start()
    out_ref[...] = dot(slots_ref[0], home[:, :feat], ((0,), (0,)), high).astype(BF16)
    done.append(pltpu.make_async_copy(out_ref, out_hbm, sem.at[4]))
    done[-1].start()
    grad_ref[...] = dot(slots_ref[1], home[:, feat:], ((0,), (0,)), high).astype(BF16)
    done.append(pltpu.make_async_copy(grad_ref, grad_hbm, sem.at[5]))
    done[-1].start()
    for copy in done:
        copy.wait()


def per_device(tokens, cotangent, expert_ids, gate_weights, w_gate, w_up, w_down):
    tok_rows, feat = tokens.shape
    wide, units = w_gate.shape
    planes = lax.axis_size("expert") // EXPERTS
    cap_rows = EXPERTS * CAP
    rows = planes * cap_rows
    half = rows // 2
    hbm = pl.BlockSpec(memory_space=pl.ANY)
    dma = pltpu.SemaphoreType.DMA
    block = (EXPERTS, SLOT, 2 * feat)
    part = cap_rows // 2
    home, slots, made = pl.pallas_call(
        kernel,
        out_shape=(
            jax.ShapeDtypeStruct(block, BF16),
            jax.ShapeDtypeStruct((2, EXPERTS * SLOT, tok_rows), F32),
            jax.ShapeDtypeStruct((units, wide), BF16),
        ),
        in_specs=[hbm] * 7,
        out_specs=(hbm, hbm, hbm),
        scratch_shapes=[
            pltpu.VMEM((2, tok_rows), jnp.int32), pltpu.VMEM((2, tok_rows), F32),
            pltpu.VMEM((tok_rows, feat), BF16), pltpu.VMEM((tok_rows, feat), BF16), dma((4,)),
            pltpu.VMEM((wide, units), BF16), pltpu.VMEM((wide, units), BF16),
            pltpu.VMEM((units, wide), BF16), dma((3,)),
            pltpu.VMEM(block, BF16), pltpu.VMEM((len(RELAYS),) + block[1:], BF16),
            pltpu.VMEM(block, BF16), dma((len(ARRIVALS),)), dma((len(ARRIVALS),)),
            pltpu.VMEM((4, 2, planes, part, 2 * feat), BF16),
            dma((2, 3)), dma((2, 3)), dma((2, 4, 3)), dma((2, 4, 3)),
            pltpu.VMEM((2, 4, half, 384), F32), pltpu.VMEM((2, 4, half // 2, 384), F32), dma((2, 4)), dma((2, 4)),
            pltpu.VMEM((2, half // 2, 384), F32),
            pltpu.VMEM((2, 3, half // 2, 384), BF16), pltpu.VMEM((2, 3, half // 2, 384), BF16),
            dma((2, 3)), dma((2, 3)),
            pltpu.VMEM((2, 4, 2, half // 2, 384), BF16), dma((2, 2, 3)), dma((2, 2, 3)), dma((2,)), dma((2,)),
            pltpu.VMEM((2, 4, half, 2 * feat), BF16),
            pltpu.VMEM((2, 3, half, 2 * feat), BF16), dma((2, 3)), dma((2, 3)),
            pltpu.VMEM((2, planes, part, 2 * feat), F32),
            pltpu.VMEM((2, 3, part, 2 * feat), BF16), pltpu.VMEM((2, 3, part, 2 * feat), BF16),
            dma((2, 3)), dma((2, 3)),
            pltpu.VMEM(block, BF16), dma((7,)), dma((7,)),
            pltpu.VMEM((2, EXPERTS * SLOT, tok_rows), F32),
            pltpu.VMEM((rows, units), BF16), pltpu.VMEM((rows, wide), BF16),
            pltpu.VMEM((units, wide), BF16), dma((3,)),
        ],
        compiler_params=pltpu.CompilerParams(collective_id=0, has_side_effects=True),
    )(expert_ids.T, gate_weights.T, tokens, cotangent, w_gate, w_up, w_down)
    return pl.pallas_call(
        finish,
        out_shape=(
            jax.ShapeDtypeStruct((tok_rows, feat), BF16),
            jax.ShapeDtypeStruct((tok_rows, feat), BF16),
            jax.ShapeDtypeStruct((units, wide), BF16),
        ),
        in_specs=[hbm] * 3,
        out_specs=(hbm, hbm, hbm),
        scratch_shapes=[
            pltpu.VMEM(block, BF16), pltpu.VMEM((2, EXPERTS * SLOT, tok_rows), F32),
            pltpu.VMEM((tok_rows, feat), BF16), pltpu.VMEM((tok_rows, feat), BF16),
            pltpu.VMEM((units, wide), BF16), dma((2,)), dma((4,)), dma((6,)),
        ],
    )(home, slots, made)


def solution(mesh):
    return jax.shard_map(
        per_device,
        mesh=mesh,
        in_specs=(
            P("expert", ("dp", "tpin", "tpout")),
            P("expert", ("dp", "tpin", "tpout")),
            P("expert", None),
            P("expert", None),
            P(("dp", "tpin"), ("expert", "tpout")),
            P(("dp", "tpin"), ("expert", "tpout")),
            P(("expert", "tpout"), ("dp", "tpin")),
        ),
        out_specs=(
            P("expert", ("dp", "tpin", "tpout")),
            P("expert", ("dp", "tpin", "tpout")),
            P(("expert", "tpout"), ("dp", "tpin")),
        ),
        check_vma=False,
    )
```
